32 devices in a mesh: seq: 8 (over y, x, core), ch: 4 (over z).
Axes of the slice: x: 2, y: 2, z: 4, core: 2. Of those that a mesh axis runs over, the one named last changes fastest.
Arguments:
- dna_features: bfloat16 [2, 512, 1280], P(None, 'seq'), may hold values from -6 to 6
- gain_a: float32 [1280], replicated, may hold values from 0.25 to 1.75
- conv_a: bfloat16 [5, 1280, 1408], P(None, 'seq', 'ch'), may hold values from -0.078125 to 0.078125
- bias_a: float32 [1408], P('ch'), may hold values from -3 to 3
- gain_b: float32 [1408], replicated, may hold values from 0.25 to 1.75
- conv_b: bfloat16 [5, 1408, 1536], P(None, 'seq', 'ch'), may hold values from -0.0625 to 0.0625
- bias_b: float32 [1536], P('ch'), may hold values from -3 to 3
- grad_out: bfloat16 [2, 128, 1536], P(None, 'seq', 'ch'), may hold values from -6 to 6
Outputs:
- pooled_out: bfloat16 [2, 128, 1536], P(None, 'seq', 'ch')
- input_grad: bfloat16 [2, 512, 1280], P(None, 'seq', 'ch')
The draws below stay inside these ranges and needn't reach their ends.
All inputs are finite; a program needn't handle non-finite values.
Results may differ from the reference program's by a relative error of at most 0.018.
Values may be sent and summed in bfloat16 or wider, within the bound.
No kernel may reach another device: no remote copies, remote signals or barrier semaphores. Data moves between devices by JAX's collectives and lax.ppermute only.
A program may use at most 128 MiB of HBM per device.

```python
import math
import jax
import jax.numpy as jnp
from jax import lax

CH_IN = 1280
CH_MID = 1408
CH_OUT = 1536
TAPS = 5
WINDOWS = 2
LEN_IN = 512
LEN_MID = 256
LEN_OUT = 128


def shard_levels(key, dims, pieces, least, top_value):
    def one(axis_at, blocks):
        draws = jax.random.uniform(jax.random.fold_in(jax.random.fold_in(key, 6), axis_at), (blocks,), jnp.float32, least / len(pieces), top_value / len(pieces))
        return jnp.repeat(jnp.exp(draws), dims[axis_at] // blocks).reshape((-1,) + (1,) * (len(dims) - axis_at - 1))

    factor_of = one(*pieces[0])
    for cut in pieces[1:]:
        factor_of = factor_of * one(*cut)
    return factor_of


def gaussian(key, extent, deviation, most, cuts=(), kind=jnp.bfloat16):
    array = jax.random.normal(key, extent, jnp.float32) * deviation
    if len(cuts) > 0:
        array = shard_levels(key, extent, cuts, -0.22, 0.18) * array
    return jnp.clip(array, min=-most, max=most).astype(kind)


def setup_inputs(seed: int = 0) -> dict:
    key_of = jax.random.split(jax.random.key(seed), 9)
    return {
        "dna_features": gaussian(key_of[0], (WINDOWS, LEN_IN, CH_IN), 1.0, 6.0, ((1, 8),)),
        "gain_a": jnp.clip(1.0 + 0.15 * jax.random.normal(key_of[1], (CH_IN,), jnp.float32), 0.25, 1.75),
        "conv_a": gaussian(key_of[2], (TAPS, CH_IN, CH_MID), (TAPS * CH_IN) ** -0.5, 0.078125, ((1, 8), (2, 4))),
        "bias_a": gaussian(key_of[3], (CH_MID,), 0.5, 3.0, ((0, 4),), jnp.float32),
        "gain_b": jnp.clip(1.0 + 0.15 * jax.random.normal(key_of[4], (CH_MID,), jnp.float32), 0.25, 1.75),
        "conv_b": gaussian(key_of[5], (TAPS, CH_MID, CH_OUT), (TAPS * CH_MID) ** -0.5, 0.0625, ((1, 8), (2, 4))),
        "bias_b": gaussian(key_of[6], (CH_OUT,), 0.5, 3.0, ((0, 4),), jnp.float32),
        "grad_out": gaussian(key_of[7], (WINDOWS, LEN_OUT, CH_OUT), 1.0, 6.0, ((1, 8), (2, 4))),
    }


EPS = 1e-06
ROOT = math.sqrt(2.0 / math.pi)

def gelu_tanh(z):
    return 0.5 * z * (1.0 + jnp.tanh(ROOT * (z + 0.044715 * z * z * z)))

def gelu_slope(z):
    t = jnp.tanh(ROOT * (z + 0.044715 * z * z * z))
    return 0.5 * (1.0 + t) + 0.5 * z * (1.0 - t * t) * ROOT * (1.0 + 3.0 * 0.044715 * z * z)

def pad_rows(v):
    return jnp.pad(v, ((0, 0), (2, 2), (0, 0)))

def pool_pairs(v):
    return v.reshape(v.shape[0], v.shape[1] // 2, 2, v.shape[2]).sum(axis=2) * 0.5

def repeat_half(v):
    return (jnp.repeat(v.astype(jnp.float32), 2, axis=1) * 0.5).astype(jnp.bfloat16)

def conv_rows(padded, weight, length):
    padded = padded.astype(jnp.float32)
    weight = weight.astype(jnp.float32)
    total = jnp.zeros((padded.shape[0], length, weight.shape[2]), jnp.float32)
    for offset in range(TAPS):
        total = total + jnp.einsum('wtc,co->wto', padded[:, offset:offset + length], weight[offset])
    return total

def conv_back(padded, weight, length):
    padded = padded.astype(jnp.float32)
    weight = weight.astype(jnp.float32)
    total = jnp.zeros((padded.shape[0], length, weight.shape[1]), jnp.float32)
    for offset in range(TAPS):
        start = 4 - offset
        total = total + jnp.einsum('wto,co->wtc', padded[:, start:start + length], weight[offset])
    return total

def norm_back(back, values, scale, gain):
    normed = values * scale
    grad_n = back * gelu_slope(normed * gain) * gain
    inner = lax.optimization_barrier(jnp.mean(grad_n * normed, axis=-1, keepdims=True))
    return scale * (grad_n - normed * inner)

def reference(dna_features, gain_a, conv_a, bias_a, gain_b, conv_b, bias_b, grad_out):
    feat = dna_features.astype(jnp.float32)
    scale_a = lax.rsqrt(lax.optimization_barrier(jnp.mean(feat * feat, axis=-1, keepdims=True)) + EPS)
    act_a = gelu_tanh(feat * scale_a * gain_a).astype(jnp.bfloat16)
    mid = pool_pairs(conv_rows(pad_rows(act_a), conv_a, LEN_IN) + bias_a).astype(jnp.bfloat16)
    mid_f = mid.astype(jnp.float32)
    scale_b = lax.rsqrt(lax.optimization_barrier(jnp.mean(mid_f * mid_f, axis=-1, keepdims=True)) + EPS)
    act_b = gelu_tanh(mid_f * scale_b * gain_b).astype(jnp.bfloat16)
    pooled_out = pool_pairs(conv_rows(pad_rows(act_b), conv_b, LEN_MID) + bias_b).astype(jnp.bfloat16)
    grad_b = repeat_half(grad_out)
    back_b = conv_back(pad_rows(grad_b), conv_b, LEN_MID)
    grad_mid = norm_back(back_b, mid_f, scale_b, gain_b).astype(jnp.bfloat16)
    grad_a = repeat_half(grad_mid)
    back_a = conv_back(pad_rows(grad_a), conv_a, LEN_IN)
    input_grad = norm_back(back_a, feat, scale_a, gain_a).astype(jnp.bfloat16)
    return (pooled_out, input_grad)
```

```python
import math

import jax
import jax.numpy as jnp
from jax import lax
from jax.sharding import PartitionSpec as P

EPS = 1e-06
ROOT = math.sqrt(2.0 / math.pi)


def with_halo(block, sides, width):
    for axis, dim in sides:
        count = lax.axis_size(axis)
        forward = [(i, i + 1) for i in range(count - 1)]
        backward = [(target, source) for source, target in forward]
        low = lax.ppermute(
            lax.slice_in_dim(block, block.shape[dim] - width, None, axis=dim), axis, forward
        )
        high = lax.ppermute(lax.slice_in_dim(block, 0, width, axis=dim), axis, backward)
        block = jnp.concatenate([low, block, high], axis=dim)
    return block


def gelu_tanh(z):
    return 0.5 * z * (1.0 + jnp.tanh(ROOT * (z + 0.044715 * z * z * z)))


def gelu_slope(z):
    t = jnp.tanh(ROOT * (z + 0.044715 * z * z * z))
    return 0.5 * (1.0 + t) + 0.5 * z * (1.0 - t * t) * ROOT * (1.0 + 3.0 * 0.044715 * z * z)


def pool_pairs(v):
    return v.reshape(v.shape[0], v.shape[1] // 2, 2, v.shape[2]).sum(axis=2) * 0.5


def repeat_half(v):
    return (jnp.repeat(v.astype(jnp.float32), 2, axis=1) * 0.5).astype(jnp.bfloat16)


def conv_rows(padded, weight, length):
    total = jnp.einsum(
        "wtc,co->wto", padded[:, 0:length], weight[0], preferred_element_type=jnp.float32
    )
    for offset in range(1, weight.shape[0]):
        total = total + jnp.einsum(
            "wtc,co->wto",
            padded[:, offset : offset + length],
            weight[offset],
            preferred_element_type=jnp.float32,
        )
    return total


def conv_back(padded, weight, length):
    total = jnp.einsum(
        "wto,co->wtc", padded[:, 4 : 4 + length], weight[0], preferred_element_type=jnp.float32
    )
    for offset in range(1, weight.shape[0]):
        start = 4 - offset
        total = total + jnp.einsum(
            "wto,co->wtc",
            padded[:, start : start + length],
            weight[offset],
            preferred_element_type=jnp.float32,
        )
    return total


def per_device(dna_features, gain_a, conv_a, bias_a, gain_b, conv_b, bias_b, grad_out):
    rows_in = dna_features.shape[1]
    rows_mid = rows_in // 2
    width_in = dna_features.shape[2]
    width_mid = gain_b.shape[0]
    share_mid = bias_a.shape[0]
    share_in = width_in // lax.axis_size("ch")
    ch_index = lax.axis_index("ch")
    whole_a, whole_b = (
        lax.all_gather(conv_a, "seq", axis=1, tiled=True),
        lax.all_gather(conv_b, "seq", axis=1, tiled=True),
    )
    feat = dna_features.astype(jnp.float32)
    scale_a = lax.rsqrt(jnp.mean(feat * feat, axis=-1, keepdims=True) + EPS)
    act_a = gelu_tanh(feat * scale_a * gain_a).astype(jnp.bfloat16)
    padded_a = with_halo(act_a, (("seq", 1),), 2)
    conv_out_a = conv_rows(padded_a, whole_a, rows_in)
    mid = pool_pairs(conv_out_a + bias_a).astype(jnp.bfloat16)
    gain_part = lax.dynamic_slice_in_dim(gain_b, ch_index * share_mid, share_mid, 0)
    mid_f = mid.astype(jnp.float32)
    squares = lax.psum(jnp.sum(mid_f * mid_f, axis=-1, keepdims=True), "ch")
    scale_b = lax.rsqrt(squares / width_mid + EPS)
    act_part = gelu_tanh(mid_f * scale_b * gain_part).astype(jnp.bfloat16)
    act_full = lax.all_gather(act_part, "ch", axis=2, tiled=True)
    padded_b = with_halo(act_full, (("seq", 1),), 2)
    conv_out_b = conv_rows(padded_b, whole_b, rows_mid)
    pooled_out = pool_pairs(conv_out_b + bias_b).astype(jnp.bfloat16)
    grad_b = repeat_half(grad_out)
    grad_pad_b = with_halo(grad_b, (("seq", 1),), 2)
    partial_b = conv_back(grad_pad_b, whole_b, rows_mid)
    back_share = lax.psum_scatter(
        partial_b.astype(jnp.bfloat16), "ch", scatter_dimension=2, tiled=True
    ).astype(jnp.float32)
    normed_b = mid_f * scale_b
    grad_n = back_share * gelu_slope(normed_b * gain_part) * gain_part
    inner_b = lax.psum(jnp.sum(grad_n * normed_b, axis=-1, keepdims=True), "ch") / width_mid
    grad_mid = (scale_b * (grad_n - normed_b * inner_b)).astype(jnp.bfloat16)
    grad_a = repeat_half(grad_mid)
    grad_pad_a = with_halo(grad_a, (("seq", 1),), 2)
    partial_a = conv_back(grad_pad_a, whole_a, rows_in)
    back_share_a = lax.psum_scatter(
        partial_a.astype(jnp.bfloat16), "ch", scatter_dimension=2, tiled=True
    ).astype(jnp.float32)
    feat_part = lax.dynamic_slice_in_dim(feat, ch_index * share_in, share_in, 2)
    gain_part_a = lax.dynamic_slice_in_dim(gain_a, ch_index * share_in, share_in, 0)
    normed_a = feat_part * scale_a
    grad_na = back_share_a * gelu_slope(normed_a * gain_part_a) * gain_part_a
    inner_a = lax.psum(jnp.sum(grad_na * normed_a, axis=-1, keepdims=True), "ch") / width_in
    input_grad = (scale_a * (grad_na - normed_a * inner_a)).astype(jnp.bfloat16)
    return (pooled_out, input_grad)


def swap(x, axis, bit):
    count = lax.axis_size(axis)
    return lax.ppermute(x, axis, [(i, i ^ bit) for i in range(count)])


def transpose_chips(x):
    chips = lax.axis_size("ch")
    pairs = []
    for chip in range(chips):
        for core in range(2):
            for layer in range(chips):
                source = (2 * chip + core) * chips + layer
                pairs.append((source, (2 * layer + core) * chips + chip))
    return lax.ppermute(x, ("seq", "ch"), pairs)


def pick(stack, index):
    return lax.dynamic_index_in_dim(stack, index, 0, keepdims=False)


def ordered(blocks, index):
    stack = jnp.stack(blocks)
    return jnp.take(stack, jnp.arange(len(blocks)) ^ index, axis=0)


def two_cores(mine, other, core):
    return jnp.where(
        core == 0,
        jnp.concatenate([mine, other], axis=-2),
        jnp.concatenate([other, mine], axis=-2),
    )


def later(v):
    return jnp.concatenate([v[..., 1:, :], jnp.zeros_like(v[..., :1, :])], axis=-2)


def earlier(v):
    return jnp.concatenate([jnp.zeros_like(v[..., :1, :]), v[..., :-1, :]], axis=-2)


def matmul(a, b):
    return jnp.einsum("rc,co->ro", a, b, preferred_element_type=jnp.float32)


def reduce_layers(parts, layer):
    low, high = layer % 2, layer // 2
    parts = parts.reshape((2, 2) + parts.shape[1:])
    kept = jnp.where(low == 0, parts[:, 0], parts[:, 1])
    sent = jnp.where(low == 0, parts[:, 1], parts[:, 0])
    kept = kept + swap(sent.astype(jnp.bfloat16), "ch", 1).astype(jnp.float32)
    sent = pick(kept, 1 - high).astype(jnp.bfloat16)
    return pick(kept, high) + swap(sent, "ch", 2).astype(jnp.float32)


def reduce_chips(parts, chip):
    total = pick(parts, chip)
    for step in range(1, parts.shape[0]):
        sent = pick(parts, chip ^ step).astype(jnp.bfloat16)
        total = total + swap(sent, "seq", 2 * step).astype(jnp.float32)
    return total


def stationary(dna_features, gain_a, conv_a, bias_a, gain_b, conv_b, bias_b, grad_out):
    f32, bf16 = jnp.float32, jnp.bfloat16
    chips = lax.axis_size("ch")
    place = lax.axis_index("seq")
    layer = lax.axis_index("ch")
    chip, core = place // 2, place % 2
    windows, rows_in, width_in = dna_features.shape
    width_mid = gain_b.shape[0]
    share_in, share_mid, share_out = width_in // chips, bias_a.shape[0], bias_b.shape[0]
    part = rows_in // 4
    block = 2 * part
    length = chips * block
    taps = conv_a.shape[0]

    whole_a = two_cores(conv_a, swap(conv_a, "seq", 1), core)
    whole_b = two_cores(conv_b, swap(conv_b, "seq", 1), core)

    feat = dna_features.astype(f32)
    scale_a = lax.rsqrt(jnp.mean(feat * feat, axis=-1, keepdims=True) + EPS)
    normed = (feat * scale_a).astype(bf16)
    planes = normed.reshape(windows, part, 4, width_in).transpose(0, 2, 1, 3)
    mine = two_cores(pick(planes, core), swap(pick(planes, 1 - core), "seq", 1), core)
    cot = two_cores(pick(grad_out, core), swap(pick(grad_out, 1 - core), "seq", 1), core)

    shares = mine.reshape(4 * block, chips, share_in).transpose(1, 0, 2)
    normed_blocks = [pick(shares, chip)]
    cot_blocks = [cot]
    for step in range(1, chips):
        normed_blocks.append(swap(pick(shares, chip ^ step), "seq", 2 * step))
        cot_blocks.append(swap(cot, "seq", 2 * step))
    normed_all = ordered(normed_blocks, chip)
    cot_all = ordered(cot_blocks, chip).reshape(length, share_out)

    gain_in = pick(gain_a.reshape(chips, share_in), chip)
    v = normed_all.reshape(chips, 4, block, share_in).transpose(1, 0, 2, 3)
    v = v.reshape(4, length, share_in).astype(f32)
    act = gelu_tanh(v * gain_in)
    pa = (0.5 * (act[0] + act[1])).astype(bf16)
    pb = (0.5 * (act[1] + act[2])).astype(bf16)
    pc = (0.5 * (act[2] + act[3])).astype(bf16)
    pd = (0.5 * (act[3] + later(act[0]))).astype(bf16)
    edge = (0.5 * act[0, :1]).astype(bf16)
    pd_early = jnp.concatenate([edge, pd[:-1]], axis=0)
    even = jnp.concatenate([earlier(pc), pd_early, pa, pb, pc], axis=1)
    odd = jnp.concatenate([pa, pb, pc, pd, later(pa)], axis=1)
    mid_part = matmul(
        jnp.concatenate([even, odd], axis=0), whole_a.reshape(taps * share_in, share_mid)
    )
    mid_part = mid_part.reshape(2, chips, block, share_mid).transpose(1, 0, 2, 3)
    mid = reduce_chips(mid_part.reshape(chips, 2 * block, share_mid), chip)
    mid = (mid + bias_a).astype(bf16)

    prod = [
        jnp.einsum("ro,co->rc", cot_all, whole_b[t], preferred_element_type=f32)
        for t in range(taps)
    ]
    back_even = later(prod[0]) + prod[1] + prod[2] + earlier(prod[3] + prod[4])
    back_odd = later(prod[0] + prod[1]) + prod[2] + prod[3] + earlier(prod[4])
    back = 0.5 * jnp.stack([back_even, back_odd])
    back = back.reshape(2, chips, block, share_mid).transpose(1, 0, 2, 3)
    back = reduce_layers(back.reshape(chips, 2 * block, share_mid), layer)
    back = transpose_chips(back.astype(bf16))

    both = jnp.concatenate([mid, back], axis=1)
    near = swap(both, "ch", 1)
    pair = jnp.stack([both, near])
    far = swap(pair, "ch", 2)
    both = ordered([pair[0], pair[1], far[0], far[1]], layer).astype(f32)
    mid_all, back_all = both[:, :, :share_mid], both[:, :, share_mid:]
    gain_mid = gain_b.reshape(chips, 1, share_mid)
    squares = jnp.sum(mid_all * mid_all, axis=(0, 2), keepdims=True)
    scale_b = lax.rsqrt(squares / width_mid + EPS)
    normed_b = mid_all * scale_b
    act_b = gelu_tanh(normed_b * gain_mid).astype(bf16)
    grad_n = back_all * gelu_slope(normed_b * gain_mid) * gain_mid
    inner_b = jnp.sum(grad_n * normed_b, axis=(0, 2), keepdims=True) / width_mid
    grad_mid = (scale_b * (grad_n - normed_b * inner_b)).astype(bf16)
    grad_mid = pick(grad_mid, layer)

    rest = [jnp.concatenate([pick(act_b, chip), grad_mid], axis=1)]
    for step in range(1, chips):
        sent = jnp.concatenate([pick(act_b, chip ^ step), grad_mid], axis=1)
        rest.append(swap(sent, "seq", 2 * step))
    rest = ordered(rest, chip).reshape(chips, 2, block, 2 * share_mid)
    rest = rest.transpose(1, 0, 2, 3).reshape(2, length, 2 * share_mid)

    u = rest[:, :, share_mid:]
    w_rows = [
        jnp.einsum("erm,cm->erc", u, whole_a[t], preferred_element_type=f32)
        for t in range(taps)
    ]
    e = [p[0] for p in w_rows]
    o = [p[1] for p in w_rows]
    grads = 0.5 * jnp.stack(
        [
            o[0] + e[1] + e[2] + earlier(o[3] + o[4]),
            o[0] + o[1] + e[2] + e[3] + earlier(o[4]),
            later(e[0]) + o[1] + o[2] + e[3] + e[4],
            later(e[0] + e[1]) + o[2] + o[3] + e[4],
        ]
    )
    grads = grads.reshape(4, chips, block, share_in).transpose(1, 0, 2, 3)
    grads = reduce_layers(grads.reshape(chips, 4 * block, share_in), layer)
    normed_q = pick(normed_all, layer).astype(f32)
    grad_n = grads * gelu_slope(normed_q * gain_in) * gain_in
    inner_a = jnp.sum(grad_n * normed_q, axis=-1)
    inner_a = inner_a + swap(inner_a, "seq", 2)
    inner_a = inner_a + swap(inner_a, "seq", 4)
    grad_n = grad_n - normed_q * (inner_a / width_in)[:, None]
    grad_n = transpose_chips(grad_n.astype(bf16)).reshape(4, 2, part, share_in)
    grad_n = grad_n.transpose(1, 0, 2, 3)
    own, other = pick(grad_n, core), swap(pick(grad_n, 1 - core), "seq", 1)
    own, other = jnp.where(core == 0, own, other), jnp.where(core == 0, other, own)
    input_grad = jnp.stack([own, other]).transpose(0, 2, 1, 3)
    input_grad = input_grad.reshape(windows, rows_in, share_in).astype(f32) * scale_a
    input_grad = input_grad.astype(bf16)

    a = rest[:, :, :share_mid].astype(f32)
    qe = (0.5 * (a[0] + a[1])).astype(bf16)
    qo = (0.5 * (a[1] + later(a[0]))).astype(bf16)
    edge = (0.5 * a[0, :1]).astype(bf16)
    qo_early = jnp.concatenate([edge, qo[:-1]], axis=0)
    cols = jnp.concatenate([earlier(qe), qo_early, qe, qo, later(qe)], axis=1)
    out = matmul(cols, whole_b.reshape(taps * share_mid, share_out))
    out = reduce_chips(out.reshape(chips, block, share_out), chip)
    out = (out + bias_b).astype(bf16).reshape(2, part, share_out)
    own, other = pick(out, core), swap(pick(out, 1 - core), "seq", 1)
    own, other = jnp.where(core == 0, own, other), jnp.where(core == 0, other, own)
    return (jnp.stack([own, other]), input_grad)


def fits(mesh_shape, args):
    places, layers = mesh_shape["seq"], mesh_shape["ch"]
    windows, rows = args[0].shape[0], args[0].shape[1]
    return places == 2 * layers and layers == 4 and windows == 2 and rows % (32 * places) == 0


def solution(mesh):
    in_specs = (
        P(None, "seq", None),
        P(),
        P(None, "seq", "ch"),
        P("ch"),
        P(),
        P(None, "seq", "ch"),
        P("ch"),
        P(None, "seq", "ch"),
    )
    out_specs = (P(None, "seq", "ch"), P(None, "seq", "ch"))

    def run(*args):
        plan = stationary if fits(mesh.shape, args) else per_device
        return jax.shard_map(
            plan, mesh=mesh, in_specs=in_specs, out_specs=out_specs, check_vma=False
        )(*args)

    return run
```

```python
import functools
import math

import jax
import jax.numpy as jnp
from jax import lax
from jax.experimental import pallas as pl
from jax.experimental.pallas import tpu as pltpu
from jax.sharding import PartitionSpec as P

EPS = 1e-06
F32, BF16 = jnp.float32, jnp.bfloat16
ROOT = math.sqrt(2.0 / math.pi)


def with_halo(block, sides, width):
    for axis, dim in sides:
        count = lax.axis_size(axis)
        forward = [(i, i + 1) for i in range(count - 1)]
        backward = [(target, source) for source, target in forward]
        low = lax.ppermute(
            lax.slice_in_dim(block, block.shape[dim] - width, None, axis=dim), axis, forward
        )
        high = lax.ppermute(lax.slice_in_dim(block, 0, width, axis=dim), axis, backward)
        block = jnp.concatenate([low, block, high], axis=dim)
    return block


def gelu_tanh(z):
    return 0.5 * z * (1.0 + jnp.tanh(ROOT * (z + 0.044715 * z * z * z)))


def gelu_slope(z):
    t = jnp.tanh(ROOT * (z + 0.044715 * z * z * z))
    return 0.5 * (1.0 + t) + 0.5 * z * (1.0 - t * t) * ROOT * (1.0 + 3.0 * 0.044715 * z * z)


def pool_pairs(v):
    return v.reshape(v.shape[0], v.shape[1] // 2, 2, v.shape[2]).sum(axis=2) * 0.5


def repeat_half(v):
    return (jnp.repeat(v.astype(jnp.float32), 2, axis=1) * 0.5).astype(jnp.bfloat16)


def conv_rows(padded, weight, length):
    total = jnp.einsum(
        "wtc,co->wto", padded[:, 0:length], weight[0], preferred_element_type=jnp.float32
    )
    for offset in range(1, weight.shape[0]):
        total = total + jnp.einsum(
            "wtc,co->wto",
            padded[:, offset : offset + length],
            weight[offset],
            preferred_element_type=jnp.float32,
        )
    return total


def conv_back(padded, weight, length):
    total = jnp.einsum(
        "wto,co->wtc", padded[:, 4 : 4 + length], weight[0], preferred_element_type=jnp.float32
    )
    for offset in range(1, weight.shape[0]):
        start = 4 - offset
        total = total + jnp.einsum(
            "wto,co->wtc",
            padded[:, start : start + length],
            weight[offset],
            preferred_element_type=jnp.float32,
        )
    return total


def per_device(dna_features, gain_a, conv_a, bias_a, gain_b, conv_b, bias_b, grad_out):
    rows_in = dna_features.shape[1]
    rows_mid = rows_in // 2
    width_in = dna_features.shape[2]
    width_mid = gain_b.shape[0]
    share_mid = bias_a.shape[0]
    share_in = width_in // lax.axis_size("ch")
    ch_index = lax.axis_index("ch")
    whole_a, whole_b = (
        lax.all_gather(conv_a, "seq", axis=1, tiled=True),
        lax.all_gather(conv_b, "seq", axis=1, tiled=True),
    )
    feat = dna_features.astype(jnp.float32)
    scale_a = lax.rsqrt(jnp.mean(feat * feat, axis=-1, keepdims=True) + EPS)
    act_a = gelu_tanh(feat * scale_a * gain_a).astype(jnp.bfloat16)
    padded_a = with_halo(act_a, (("seq", 1),), 2)
    conv_out_a = conv_rows(padded_a, whole_a, rows_in)
    mid = pool_pairs(conv_out_a + bias_a).astype(jnp.bfloat16)
    gain_part = lax.dynamic_slice_in_dim(gain_b, ch_index * share_mid, share_mid, 0)
    mid_f = mid.astype(jnp.float32)
    squares = lax.psum(jnp.sum(mid_f * mid_f, axis=-1, keepdims=True), "ch")
    scale_b = lax.rsqrt(squares / width_mid + EPS)
    act_part = gelu_tanh(mid_f * scale_b * gain_part).astype(jnp.bfloat16)
    act_full = lax.all_gather(act_part, "ch", axis=2, tiled=True)
    padded_b = with_halo(act_full, (("seq", 1),), 2)
    conv_out_b = conv_rows(padded_b, whole_b, rows_mid)
    pooled_out = pool_pairs(conv_out_b + bias_b).astype(jnp.bfloat16)
    grad_b = repeat_half(grad_out)
    grad_pad_b = with_halo(grad_b, (("seq", 1),), 2)
    partial_b = conv_back(grad_pad_b, whole_b, rows_mid)
    back_share = lax.psum_scatter(
        partial_b.astype(jnp.bfloat16), "ch", scatter_dimension=2, tiled=True
    ).astype(jnp.float32)
    normed_b = mid_f * scale_b
    grad_n = back_share * gelu_slope(normed_b * gain_part) * gain_part
    inner_b = lax.psum(jnp.sum(grad_n * normed_b, axis=-1, keepdims=True), "ch") / width_mid
    grad_mid = (scale_b * (grad_n - normed_b * inner_b)).astype(jnp.bfloat16)
    grad_a = repeat_half(grad_mid)
    grad_pad_a = with_halo(grad_a, (("seq", 1),), 2)
    partial_a = conv_back(grad_pad_a, whole_a, rows_in)
    back_share_a = lax.psum_scatter(
        partial_a.astype(jnp.bfloat16), "ch", scatter_dimension=2, tiled=True
    ).astype(jnp.float32)
    feat_part = lax.dynamic_slice_in_dim(feat, ch_index * share_in, share_in, 2)
    gain_part_a = lax.dynamic_slice_in_dim(gain_a, ch_index * share_in, share_in, 0)
    normed_a = feat_part * scale_a
    grad_na = back_share_a * gelu_slope(normed_a * gain_part_a) * gain_part_a
    inner_a = lax.psum(jnp.sum(grad_na * normed_a, axis=-1, keepdims=True), "ch") / width_in
    input_grad = (scale_a * (grad_na - normed_a * inner_a)).astype(jnp.bfloat16)
    return (pooled_out, input_grad)


def swap(x, axis, bit):
    count = lax.axis_size(axis)
    return lax.ppermute(x, axis, [(i, i ^ bit) for i in range(count)])


def transpose_chips(x, flip):
    chips = lax.axis_size("ch")
    pairs = []
    for chip in range(chips):
        for core in range(2):
            for layer in range(chips):
                source = (2 * chip + core) * chips + layer
                pairs.append((source, (2 * layer + (core ^ flip)) * chips + chip))
    return lax.ppermute(x, ("seq", "ch"), pairs)


def call(body, outs, where, operands, scratch=(), flops=0):
    total = sum(math.prod(s) * jnp.dtype(t).itemsize for s, t in outs)
    total += sum(a.size * a.dtype.itemsize for a in operands)
    return pl.pallas_call(
        body,
        out_shape=[jax.ShapeDtypeStruct(s, t) for s, t in outs],
        in_specs=[pl.BlockSpec(memory_space=pltpu.SMEM)]
        + [pl.BlockSpec(memory_space=pltpu.VMEM)] * len(operands),
        out_specs=[pl.BlockSpec(memory_space=pltpu.VMEM)] * len(outs),
        scratch_shapes=[pltpu.VMEM(s, t) for s, t in scratch],
        cost_estimate=pl.CostEstimate(flops=flops, bytes_accessed=total, transcendentals=0),
    )(where, *operands)


def later(v):
    rows = lax.broadcasted_iota(jnp.int32, v.shape, 0)
    return jnp.where(rows == v.shape[0] - 1, 0.0, pltpu.roll(v, v.shape[0] - 1, 0))


def earlier(v):
    rows = lax.broadcasted_iota(jnp.int32, v.shape, 0)
    return jnp.where(rows == 0, 0.0, pltpu.roll(v, 1, 0))


def dot(a, b):
    return jnp.dot(a, b, preferred_element_type=F32)


def dot_t(a, b):
    return lax.dot_general(a, b, (((1,), (1,)), ((), ())), preferred_element_type=F32)


def join_cores(whole, mine, other, core):
    half = mine.shape[1]
    for t in range(mine.shape[0]):
        whole[t, pl.ds(pl.multiple_of(core * half, 16), half), :] = mine[t]
        whole[t, pl.ds(pl.multiple_of((1 - core) * half, 16), half), :] = other[t]


def pack_kernel(where, dna, dna_other, cot, cot_other, b0, b1, b2, b3, rows, shares):
    chip, core = where[0], where[1]
    part = dna.shape[1] // 4
    share = dna.shape[2] // 4
    for source, position in ((dna[core], core), (dna_other[...], 1 - core)):
        v = source.astype(F32)
        v = v * lax.rsqrt(jnp.mean(v * v, axis=-1, keepdims=True) + EPS)
        tiles = rows.shape[0]
        for tile in range(tiles):
            rows[tile] = v[:, 128 * tile : 128 * tile + 128]
        for plane in range(4):
            at = pl.multiple_of(2 * part * plane + part * position, 16)
            taken = [rows[tile, pl.ds(plane, part, stride=4), :] for tile in range(tiles)]
            taken = jnp.concatenate(taken, axis=1).astype(BF16)
            for j in range(4):
                shares[j, pl.ds(at, part), :] = taken[:, share * j : share * j + share]
    at = pl.multiple_of(part * core, 16)
    far = pl.multiple_of(part * (1 - core), 16)
    for step, out in enumerate((b0, b1, b2, b3)):
        out[0 : 8 * part, 0:share] = shares[chip ^ step]
        out[pl.ds(8 * part + at, part), :] = cot[core]
        out[pl.ds(8 * part + far, part), :] = cot_other[...]


def first_kernel(
    where, b0, b1, b2, b3, gain, wa, wa_o, wb, wb_o,
    own, s1, s2, s3, planes, cots, cols, whole_a, whole_b, total,
):
    chip, core = where[0], where[1]
    block = b0.shape[0] // 5
    share = gain.shape[2]
    join_cores(whole_a, wa, wa_o, core)
    join_cores(whole_b, wb, wb_o, core)
    for step, b in enumerate((b0, b1, b2, b3)):
        at = pl.multiple_of(block * (chip ^ step), 32)
        for plane in range(4):
            planes[plane, pl.ds(at, block), :] = b[block * plane : block * plane + block, 0:share]
        cots[pl.ds(at, block), :] = b[4 * block : 5 * block, :]
    length = 4 * block
    g = gain[chip]
    act = [gelu_tanh(planes[plane].astype(F32) * g) for plane in range(4)]
    pa = 0.5 * (act[0] + act[1])
    pb = 0.5 * (act[1] + act[2])
    pc = 0.5 * (act[2] + act[3])
    pd = 0.5 * (act[3] + later(act[0]))
    pd_early = 0.5 * (earlier(act[3]) + act[0])
    even = (earlier(pc), pd_early, pa, pb, pc)
    odd = (pa, pb, pc, pd, later(pa))
    for t in range(5):
        cols[t, 0:length, :] = even[t].astype(BF16)
        cols[t, length : 2 * length, :] = odd[t].astype(BF16)
    acc = dot(cols[0], whole_a[0])
    for t in range(1, 5):
        acc = acc + dot(cols[t], whole_a[t])
    total[0] = acc[0:length]
    total[1] = acc[length : 2 * length]
    c = cots[...]
    p = [dot_t(c, whole_b[t]) for t in range(5)]
    total[2] = 0.5 * (later(p[0]) + p[1] + p[2] + earlier(p[3] + p[4]))
    total[3] = 0.5 * (later(p[0] + p[1]) + p[2] + p[3] + earlier(p[4]))
    for step, out in enumerate((own, s1, s2, s3)):
        at = pl.multiple_of(block * (chip ^ step), 32)
        for kind in range(2):
            for half in range(2):
                out[kind, block * half : block * half + block, :] = total[
                    2 * kind + half, pl.ds(at, block), :
                ].astype(out.dtype)


def second_kernel(where, own, r1, r2, r3, bias, mid, send, kept, back):
    chip, low = where[0], where[2] % 2
    value = own[0] + r1[0].astype(F32) + r2[0].astype(F32) + r3[0].astype(F32) + bias[...]
    mid[...] = value.astype(BF16)
    send[0] = value.astype(BF16)
    back[chip] = own[1]
    for step, r in ((1, r1), (2, r2), (3, r3)):
        back[chip ^ step] = r[1].astype(F32)
    for high in range(2):
        send[1 + high] = back[2 * high + 1 - low].astype(BF16)
        kept[high] = back[2 * high + low]


def third_kernel(where, mid, near, kept, send, keep):
    high = where[2] // 2
    send[0] = mid[...]
    send[1] = near[0]
    send[2] = (kept[1 - high] + near[2 - high].astype(F32)).astype(BF16)
    keep[...] = kept[high] + near[1 + high].astype(F32)


def fourth_kernel(
    where, pair, far, keep, gain, a0, a1, a2, a3, grad_n, normed, scale, inner, mids, acts
):
    chip, layer = where[0], where[2]
    mids[layer] = pair[0].astype(F32)
    mids[layer ^ 1] = pair[1].astype(F32)
    mids[layer ^ 2] = far[0].astype(F32)
    mids[layer ^ 3] = far[1].astype(F32)
    squares = sum(mids[j] * mids[j] for j in range(4))
    width = 4 * gain.shape[2]
    root = lax.rsqrt(jnp.sum(squares, axis=-1, keepdims=True) / width + EPS)
    for j in range(4):
        acts[j] = gelu_tanh(mids[j] * root * gain[j]).astype(BF16)
    for step, out in enumerate((a0, a1, a2, a3)):
        out[...] = acts[chip ^ step]
    n = mids[layer] * root
    g = gain[layer]
    back = keep[...] + far[2].astype(F32)
    grad = back * gelu_slope(n * g) * g
    grad_n[...] = grad
    normed[...] = n
    scale[...] = jnp.broadcast_to(root, scale.shape)
    inner[...] = jnp.broadcast_to(jnp.sum(grad * n, axis=-1, keepdims=True), inner.shape)


def fifth_kernel(where, a0, a1, a2, a3, grad_n, normed, scale, i0, i1, t0, t1, t2, t3, *, width):
    inner = (i0[:, 0:1] + i1[:, 0:1]) * (1.0 / width)
    grad = (scale[:, 0:1] * (grad_n[...] - normed[...] * inner)).astype(BF16)
    for a, t in ((a0, t0), (a1, t1), (a2, t2), (a3, t3)):
        t[0] = a[...]
        t[1] = grad


def sixth_kernel(where, t0, t1, t2, t3, wa, wa_o, send, kept, rows, whole_a, total):
    chip, core, low = where[0], where[1], where[2] % 2
    block = t0.shape[1] // 2
    length = 4 * block
    join_cores(whole_a, wa, wa_o, core)
    for step, t in enumerate((t0, t1, t2, t3)):
        at = pl.multiple_of(block * (chip ^ step), 32)
        for half in range(2):
            rows[pl.ds(pl.multiple_of(length * half + at, 32), block), :] = t[
                1, block * half : block * half + block, :
            ]
    u = rows[...]
    p = [dot_t(u, whole_a[t]) for t in range(5)]
    e = [v[0:length] for v in p]
    o = [v[length : 2 * length] for v in p]
    total[0] = 0.5 * (o[0] + e[1] + e[2] + earlier(o[3] + o[4]))
    total[1] = 0.5 * (o[0] + o[1] + e[2] + e[3] + earlier(o[4]))
    total[2] = 0.5 * (later(e[0]) + o[1] + o[2] + e[3] + e[4])
    total[3] = 0.5 * (later(e[0] + e[1]) + o[2] + o[3] + e[4])
    for high in range(2):
        away = pl.multiple_of(block * (2 * high + 1 - low), 32)
        here = pl.multiple_of(block * (2 * high + low), 32)
        for plane in range(4):
            at = slice(block * plane, block * plane + block)
            send[high, at, :] = total[plane, pl.ds(away, block), :].astype(BF16)
            kept[high, at, :] = total[plane, pl.ds(here, block), :]


def out_kernel(where, t0, t1, t2, t3, wb, wb_o, own, s1, s2, s3, rows, whole_b, total):
    chip, core = where[0], where[1]
    block = t0.shape[1] // 2
    join_cores(whole_b, wb, wb_o, core)
    for step, t in enumerate((t0, t1, t2, t3)):
        at = pl.multiple_of(block * (chip ^ step), 32)
        for half in range(2):
            rows[half, pl.ds(at, block), :] = t[0, block * half : block * half + block, :].astype(F32)
    even, odd = rows[0], rows[1]
    qe = 0.5 * (even + odd)
    qo = 0.5 * (odd + later(even))
    qo_early = 0.5 * (earlier(odd) + even)
    cols = (earlier(qe), qo_early, qe, qo, later(qe))
    acc = dot(cols[0].astype(BF16), whole_b[0])
    for t in range(1, 5):
        acc = acc + dot(cols[t].astype(BF16), whole_b[t])
    total[...] = acc
    for step, out in enumerate((own, s1, s2, s3)):
        at = pl.multiple_of(block * (chip ^ step), 32)
        out[...] = total[pl.ds(at, block), :].astype(out.dtype)


def add_out_kernel(where, own, r1, r2, r3, bias, mine, send, total):
    core = where[1]
    part = own.shape[0] // 2
    value = own[...] + r1[...].astype(F32) + r2[...].astype(F32) + r3[...].astype(F32)
    total[...] = (value + bias[...]).astype(BF16)
    mine[...] = total[pl.ds(pl.multiple_of(part * core, 16), part), :]
    send[...] = total[pl.ds(pl.multiple_of(part * (1 - core), 16), part), :]


def put_out_kernel(where, mine, other, out):
    core = where[1]
    out[core] = mine[...]
    out[1 - core] = other[...]


def seventh_kernel(where, kept, near, send, keep):
    high = where[2] // 2
    send[...] = (kept[1 - high] + near[1 - high].astype(F32)).astype(BF16)
    keep[...] = kept[high] + near[high].astype(F32)


def eighth_kernel(where, keep, far, b0, b1, b2, b3, gain, grad_n, normed, inner):
    chip, layer = where[0], where[2]
    rows, share = keep.shape
    step = chip ^ layer
    low = jnp.where(step == 0, b0[0:rows, 0:share], b1[0:rows, 0:share])
    high = jnp.where(step == 2, b2[0:rows, 0:share], b3[0:rows, 0:share])
    n = jnp.where(step < 2, low, high).astype(F32)
    g = gain[chip]
    back = keep[...] + far[...].astype(F32)
    grad = back * gelu_slope(n * g) * g
    grad_n[...] = grad
    normed[...] = n
    inner[...] = jnp.broadcast_to(jnp.sum(grad * n, axis=-1, keepdims=True), inner.shape)


def ninth_kernel(where, grad_n, normed, i0, i1, same, cross, *, width):
    core = where[1]
    block = grad_n.shape[0] // 4
    part = block // 2
    inner = (i0[:, 0:1] + i1[:, 0:1]) * (1.0 / width)
    grad = grad_n[...] - normed[...] * inner
    for plane in range(4):
        at = slice(part * plane, part * plane + part)
        lower = grad[block * plane : block * plane + part].astype(BF16)
        upper = grad[block * plane + part : block * plane + block].astype(BF16)
        same[at, :] = jnp.where(core == 0, lower, upper)
        cross[at, :] = jnp.where(core == 0, upper, lower)


def last_kernel(where, same, cross, dna, out, rows):
    core = where[1]
    part = dna.shape[1] // 4
    for x, window in ((same, core), (cross, 1 - core)):
        v = dna[window].astype(F32)
        root = lax.rsqrt(jnp.mean(v * v, axis=-1, keepdims=True) + EPS)
        share = x.shape[1]
        for plane in range(4):
            taken = x[part * plane : part * plane + part, :].astype(F32)
            for tile in range(rows.shape[0]):
                lanes = min(128, share - 128 * tile)
                rows[tile, pl.ds(plane, part, stride=4), 0:lanes] = taken[
                    :, 128 * tile : 128 * tile + lanes
                ]
        whole = jnp.concatenate([rows[tile] for tile in range(rows.shape[0])], axis=1)
        out[window] = (whole[:, 0:share] * root).astype(BF16)


def stationary(dna_features, gain_a, conv_a, bias_a, gain_b, conv_b, bias_b, grad_out):
    chips = lax.axis_size("ch")
    place = lax.axis_index("seq")
    layer = lax.axis_index("ch")
    chip, core = place // 2, place % 2
    where = jnp.stack([chip, core, layer]).astype(jnp.int32)
    windows, rows_in, width_in = dna_features.shape
    width_mid = gain_b.shape[0]
    share_in, share_mid, share_out = width_in // chips, bias_a.shape[0], bias_b.shape[0]
    part = rows_in // 4
    block = 2 * part
    length = chips * block
    taps = conv_a.shape[0]
    gain_in = gain_a.reshape(chips, 1, share_in)
    gain_mid = gain_b.reshape(chips, 1, share_mid)
    steps = range(1, chips)

    dna_other = swap(lax.dynamic_index_in_dim(dna_features, 1 - core, 0, False), "seq", 1)
    cot_other = swap(lax.dynamic_index_in_dim(grad_out, 1 - core, 0, False), "seq", 1)
    other_a = swap(conv_a, "seq", 1)
    other_b = swap(conv_b, "seq", 1)

    packed = ((5 * block, share_out), BF16)
    blocks = call(
        pack_kernel,
        [packed] * 4,
        where,
        (dna_features, dna_other, grad_out, cot_other),
        [((width_in // 128, rows_in, 128), F32), ((chips, 4 * block, share_in), BF16)],
    )
    blocks = [blocks[0]] + [swap(blocks[d], "seq", 2 * d) for d in steps]

    pair = (2, 2 * block, share_mid)
    sums = call(
        first_kernel,
        [(pair, F32)] + [(pair, BF16)] * 3,
        where,
        (*blocks, gain_in, conv_a, other_a, conv_b, other_b),
        [
            ((4, length, share_in), BF16),
            ((length, share_out), BF16),
            ((taps, 2 * length, share_in), BF16),
            ((taps, share_in, share_mid), BF16),
            ((taps, share_mid, share_out), BF16),
            ((4, length, share_mid), F32),
        ],
    )
    sums = [sums[0]] + [swap(sums[d], "seq", 2 * d) for d in steps]
    one = (2 * block, share_mid)
    mid, send, kept = call(
        second_kernel,
        [(one, BF16), ((3,) + one, BF16), ((2,) + one, F32)],
        where,
        (*sums, bias_a.reshape(1, share_mid)),
        [((chips,) + one, F32)],
    )
    near = swap(send, "ch", 1)
    pair_mid, keep = call(
        third_kernel, [((3,) + one, BF16), (one, F32)], where, (mid, near, kept)
    )
    far = swap(pair_mid, "ch", 2)
    lane = (2 * block, 128)
    *acts, grad_n, normed, scale, inner = call(
        fourth_kernel,
        [(one, BF16)] * 4 + [(one, F32), (one, F32), (lane, F32), (lane, F32)],
        where,
        (pair_mid, far, keep, gain_mid),
        [((chips,) + one, F32), ((chips,) + one, BF16)],
    )
    inner = inner + swap(inner, "ch", 1)
    inner_far = swap(inner, "ch", 2)
    rest = call(
        functools.partial(fifth_kernel, width=width_mid),
        [(pair, BF16)] * 4,
        where,
        (*acts, grad_n, normed, scale, inner, inner_far),
    )
    rest = [rest[0]] + [swap(rest[d], "seq", 2 * d) for d in steps]

    quarter = (4 * block, share_in)
    send, kept = call(
        sixth_kernel,
        [((2,) + quarter, BF16), ((2,) + quarter, F32)],
        where,
        (*rest, conv_a, other_a),
        [
            ((2 * length, share_mid), BF16),
            ((taps, share_in, share_mid), BF16),
            ((4, length, share_in), F32),
        ],
    )
    near = swap(send, "ch", 1)
    outs = call(
        out_kernel,
        [((block, share_out), F32)] + [((block, share_out), BF16)] * 3,
        where,
        (*rest, conv_b, other_b),
        [
            ((2, length, share_mid), F32),
            ((taps, share_mid, share_out), BF16),
            ((length, share_out), F32),
        ],
    )
    send, keep = call(seventh_kernel, [(quarter, BF16), (quarter, F32)], where, (kept, near))
    far = swap(send, "ch", 2)
    outs = [outs[0]] + [swap(outs[d], "seq", 2 * d) for d in steps]
    lane = (4 * block, 128)
    grad_n, normed, inner = call(
        eighth_kernel,
        [(quarter, F32), (quarter, F32), (lane, F32)],
        where,
        (keep, far, *blocks, gain_in),
    )
    inner = inner + swap(inner, "seq", 2)
    inner_far = swap(inner, "seq", 4)
    same, cross = call(
        functools.partial(ninth_kernel, width=width_in),
        [((4 * part, share_in), BF16)] * 2,
        where,
        (grad_n, normed, inner, inner_far),
    )
    same, cross = transpose_chips(same, 0), transpose_chips(cross, 1)

    mine, send = call(
        add_out_kernel,
        [((part, share_out), BF16)] * 2,
        where,
        (*outs, bias_b.reshape(1, share_out)),
        [((block, share_out), BF16)],
    )
    other = swap(send, "seq", 1)
    (pooled_out,) = call(
        put_out_kernel, [(grad_out.shape, BF16)], where, (mine, other)
    )
    (input_grad,) = call(
        last_kernel,
        [((windows, rows_in, share_in), BF16)],
        where,
        (same, cross, dna_features),
        [((-(-share_in // 128), rows_in, 128), F32)],
    )
    return (pooled_out, input_grad)


def fits(mesh_shape, args):
    places, layers = mesh_shape["seq"], mesh_shape["ch"]
    windows, rows = args[0].shape[0], args[0].shape[1]
    return places == 2 * layers and layers == 4 and windows == 2 and rows == 64 * places


def solution(mesh):
    in_specs = (
        P(None, "seq", None),
        P(),
        P(None, "seq", "ch"),
        P("ch"),
        P(),
        P(None, "seq", "ch"),
        P("ch"),
        P(None, "seq", "ch"),
    )
    out_specs = (P(None, "seq", "ch"), P(None, "seq", "ch"))
    def run(*args):
        plan = stationary if fits(mesh.shape, args) else per_device
        return jax.shard_map(
            plan, mesh=mesh, in_specs=in_specs, out_specs=out_specs, check_vma=False
        )(*args)

    return run
```

```python
import functools
import math

import jax
import jax.numpy as jnp
from jax import lax
from jax.experimental import pallas as pl
from jax.experimental.pallas import tpu as pltpu
from jax.sharding import PartitionSpec as P

EPS = 1e-06
F32, BF16 = jnp.float32, jnp.bfloat16
ROOT = math.sqrt(2.0 / math.pi)


def with_halo(block, sides, width):
    for axis, dim in sides:
        count = lax.axis_size(axis)
        forward = [(i, i + 1) for i in range(count - 1)]
        backward = [(target, source) for source, target in forward]
        low = lax.ppermute(
            lax.slice_in_dim(block, block.shape[dim] - width, None, axis=dim), axis, forward
        )
        high = lax.ppermute(lax.slice_in_dim(block, 0, width, axis=dim), axis, backward)
        block = jnp.concatenate([low, block, high], axis=dim)
    return block


def gelu_tanh(z):
    return 0.5 * z * (1.0 + jnp.tanh(ROOT * (z + 0.044715 * z * z * z)))


def gelu_slope(z):
    t = jnp.tanh(ROOT * (z + 0.044715 * z * z * z))
    return 0.5 * (1.0 + t) + 0.5 * z * (1.0 - t * t) * ROOT * (1.0 + 3.0 * 0.044715 * z * z)


def pool_pairs(v):
    return v.reshape(v.shape[0], v.shape[1] // 2, 2, v.shape[2]).sum(axis=2) * 0.5


def repeat_half(v):
    return (jnp.repeat(v.astype(jnp.float32), 2, axis=1) * 0.5).astype(jnp.bfloat16)


def conv_rows(padded, weight, length):
    total = jnp.einsum(
        "wtc,co->wto", padded[:, 0:length], weight[0], preferred_element_type=jnp.float32
    )
    for offset in range(1, weight.shape[0]):
        total = total + jnp.einsum(
            "wtc,co->wto",
            padded[:, offset : offset + length],
            weight[offset],
            preferred_element_type=jnp.float32,
        )
    return total


def conv_back(padded, weight, length):
    total = jnp.einsum(
        "wto,co->wtc", padded[:, 4 : 4 + length], weight[0], preferred_element_type=jnp.float32
    )
    for offset in range(1, weight.shape[0]):
        start = 4 - offset
        total = total + jnp.einsum(
            "wto,co->wtc",
            padded[:, start : start + length],
            weight[offset],
            preferred_element_type=jnp.float32,
        )
    return total


def per_device(dna_features, gain_a, conv_a, bias_a, gain_b, conv_b, bias_b, grad_out):
    rows_in = dna_features.shape[1]
    rows_mid = rows_in // 2
    width_in = dna_features.shape[2]
    width_mid = gain_b.shape[0]
    share_mid = bias_a.shape[0]
    share_in = width_in // lax.axis_size("ch")
    ch_index = lax.axis_index("ch")
    whole_a, whole_b = (
        lax.all_gather(conv_a, "seq", axis=1, tiled=True),
        lax.all_gather(conv_b, "seq", axis=1, tiled=True),
    )
    feat = dna_features.astype(jnp.float32)
    scale_a = lax.rsqrt(jnp.mean(feat * feat, axis=-1, keepdims=True) + EPS)
    act_a = gelu_tanh(feat * scale_a * gain_a).astype(jnp.bfloat16)
    padded_a = with_halo(act_a, (("seq", 1),), 2)
    conv_out_a = conv_rows(padded_a, whole_a, rows_in)
    mid = pool_pairs(conv_out_a + bias_a).astype(jnp.bfloat16)
    gain_part = lax.dynamic_slice_in_dim(gain_b, ch_index * share_mid, share_mid, 0)
    mid_f = mid.astype(jnp.float32)
    squares = lax.psum(jnp.sum(mid_f * mid_f, axis=-1, keepdims=True), "ch")
    scale_b = lax.rsqrt(squares / width_mid + EPS)
    act_part = gelu_tanh(mid_f * scale_b * gain_part).astype(jnp.bfloat16)
    act_full = lax.all_gather(act_part, "ch", axis=2, tiled=True)
    padded_b = with_halo(act_full, (("seq", 1),), 2)
    conv_out_b = conv_rows(padded_b, whole_b, rows_mid)
    pooled_out = pool_pairs(conv_out_b + bias_b).astype(jnp.bfloat16)
    grad_b = repeat_half(grad_out)
    grad_pad_b = with_halo(grad_b, (("seq", 1),), 2)
    partial_b = conv_back(grad_pad_b, whole_b, rows_mid)
    back_share = lax.psum_scatter(
        partial_b.astype(jnp.bfloat16), "ch", scatter_dimension=2, tiled=True
    ).astype(jnp.float32)
    normed_b = mid_f * scale_b
    grad_n = back_share * gelu_slope(normed_b * gain_part) * gain_part
    inner_b = lax.psum(jnp.sum(grad_n * normed_b, axis=-1, keepdims=True), "ch") / width_mid
    grad_mid = (scale_b * (grad_n - normed_b * inner_b)).astype(jnp.bfloat16)
    grad_a = repeat_half(grad_mid)
    grad_pad_a = with_halo(grad_a, (("seq", 1),), 2)
    partial_a = conv_back(grad_pad_a, whole_a, rows_in)
    back_share_a = lax.psum_scatter(
        partial_a.astype(jnp.bfloat16), "ch", scatter_dimension=2, tiled=True
    ).astype(jnp.float32)
    feat_part = lax.dynamic_slice_in_dim(feat, ch_index * share_in, share_in, 2)
    gain_part_a = lax.dynamic_slice_in_dim(gain_a, ch_index * share_in, share_in, 0)
    normed_a = feat_part * scale_a
    grad_na = back_share_a * gelu_slope(normed_a * gain_part_a) * gain_part_a
    inner_a = lax.psum(jnp.sum(grad_na * normed_a, axis=-1, keepdims=True), "ch") / width_in
    input_grad = (scale_a * (grad_na - normed_a * inner_a)).astype(jnp.bfloat16)
    return (pooled_out, input_grad)


def swap(x, axis, bit):
    count = lax.axis_size(axis)
    return lax.ppermute(x, axis, [(i, i ^ bit) for i in range(count)])


def transpose_chips(x, flip):
    chips = lax.axis_size("ch")
    pairs = []
    for chip in range(chips):
        for core in range(2):
            for layer in range(chips):
                source = (2 * chip + core) * chips + layer
                pairs.append((source, (2 * layer + (core ^ flip)) * chips + chip))
    return lax.ppermute(x, ("seq", "ch"), pairs)


def call(body, outs, where, operands, scratch=(), flops=0, grant=16 << 20):
    total = sum(math.prod(s) * jnp.dtype(t).itemsize for s, t in outs)
    total += sum(a.size * a.dtype.itemsize for a in operands)
    return pl.pallas_call(
        body,
        out_shape=[jax.ShapeDtypeStruct(s, t) for s, t in outs],
        in_specs=[pl.BlockSpec(memory_space=pltpu.SMEM)]
        + [pl.BlockSpec(memory_space=pltpu.VMEM)] * len(operands),
        out_specs=[pl.BlockSpec(memory_space=pltpu.VMEM)] * len(outs),
        scratch_shapes=[pltpu.VMEM(s, t) for s, t in scratch],
        compiler_params=pltpu.CompilerParams(vmem_limit_bytes=grant),
        cost_estimate=pl.CostEstimate(flops=flops, bytes_accessed=total, transcendentals=0),
    )(where, *operands)


def later(v):
    rows = lax.broadcasted_iota(jnp.int32, v.shape, 0)
    return jnp.where(rows == v.shape[0] - 1, 0.0, pltpu.roll(v, v.shape[0] - 1, 0))


def earlier(v):
    rows = lax.broadcasted_iota(jnp.int32, v.shape, 0)
    return jnp.where(rows == 0, 0.0, pltpu.roll(v, 1, 0))


def dot(a, b):
    return jnp.dot(a, b, preferred_element_type=F32)


def dot_t(a, b):
    return lax.dot_general(a, b, (((1,), (1,)), ((), ())), preferred_element_type=F32)


def join_cores(whole, mine, other, core):
    half = mine.shape[1]
    for t in range(mine.shape[0]):
        whole[t, pl.ds(pl.multiple_of(core * half, 16), half), :] = mine[t]
        whole[t, pl.ds(pl.multiple_of((1 - core) * half, 16), half), :] = other[t]


def pack_kernel(where, dna, dna_other, cot, cot_other, b0, b1, b2, b3, rows, shares):
    chip, core = where[0], where[1]
    part = dna.shape[1] // 4
    share = dna.shape[2] // 4
    for source, position in ((dna[core], core), (dna_other[...], 1 - core)):
        v = source.astype(F32)
        v = v * lax.rsqrt(jnp.mean(v * v, axis=-1, keepdims=True) + EPS)
        tiles = rows.shape[0]
        for tile in range(tiles):
            rows[tile] = v[:, 128 * tile : 128 * tile + 128]
        for plane in range(4):
            at = pl.multiple_of(2 * part * plane + part * position, 16)
            taken = [rows[tile, pl.ds(plane, part, stride=4), :] for tile in range(tiles)]
            taken = jnp.concatenate(taken, axis=1).astype(BF16)
            for j in range(4):
                shares[j, pl.ds(at, part), :] = taken[:, share * j : share * j + share]
    at = pl.multiple_of(part * core, 16)
    far = pl.multiple_of(part * (1 - core), 16)
    for step, out in enumerate((b0, b1, b2, b3)):
        out[0 : 8 * part, 0:share] = shares[chip ^ step]
        out[pl.ds(8 * part + at, part), :] = cot[core]
        out[pl.ds(8 * part + far, part), :] = cot_other[...]


def first_kernel(
    where, b0, b1, b2, b3, gain, wa, wa_o, wb, wb_o,
    own, s1, s2, s3, planes, cots, cols, whole_a, whole_b, total,
):
    chip, core = where[0], where[1]
    block = b0.shape[0] // 5
    share = gain.shape[2]
    join_cores(whole_a, wa, wa_o, core)
    join_cores(whole_b, wb, wb_o, core)
    for step, b in enumerate((b0, b1, b2, b3)):
        at = pl.multiple_of(block * (chip ^ step), 32)
        for plane in range(4):
            planes[plane, pl.ds(at, block), :] = b[block * plane : block * plane + block, 0:share]
        cots[pl.ds(at, block), :] = b[4 * block : 5 * block, :]
    length = 4 * block
    g = gain[chip]
    act = [gelu_tanh(planes[plane].astype(F32) * g) for plane in range(4)]
    pa = 0.5 * (act[0] + act[1])
    pb = 0.5 * (act[1] + act[2])
    pc = 0.5 * (act[2] + act[3])
    pd = 0.5 * (act[3] + later(act[0]))
    pd_early = 0.5 * (earlier(act[3]) + act[0])
    even = (earlier(pc), pd_early, pa, pb, pc)
    odd = (pa, pb, pc, pd, later(pa))
    for t in range(5):
        cols[t, 0:length, :] = even[t].astype(BF16)
        cols[t, length : 2 * length, :] = odd[t].astype(BF16)
    acc = dot(cols[0], whole_a[0])
    for t in range(1, 5):
        acc = acc + dot(cols[t], whole_a[t])
    total[0] = acc[0:length]
    total[1] = acc[length : 2 * length]
    c = cots[...]
    p = [dot_t(c, whole_b[t]) for t in range(5)]
    total[2] = 0.5 * (later(p[0]) + p[1] + p[2] + earlier(p[3] + p[4]))
    total[3] = 0.5 * (later(p[0] + p[1]) + p[2] + p[3] + earlier(p[4]))
    for step, out in enumerate((own, s1, s2, s3)):
        at = pl.multiple_of(block * (chip ^ step), 32)
        for kind in range(2):
            for half in range(2):
                out[kind, block * half : block * half + block, :] = total[
                    2 * kind + half, pl.ds(at, block), :
                ].astype(out.dtype)


def second_kernel(where, own, r1, r2, r3, bias, mid, send, kept, back):
    chip, low = where[0], where[2] % 2
    value = own[0] + r1[0].astype(F32) + r2[0].astype(F32) + r3[0].astype(F32) + bias[...]
    mid[...] = value.astype(BF16)
    send[0] = value.astype(BF16)
    back[chip] = own[1]
    for step, r in ((1, r1), (2, r2), (3, r3)):
        back[chip ^ step] = r[1].astype(F32)
    for high in range(2):
        send[1 + high] = back[2 * high + 1 - low].astype(BF16)
        kept[high] = back[2 * high + low]


def third_kernel(where, mid, near, kept, send, keep):
    high = where[2] // 2
    send[0] = mid[...]
    send[1] = near[0]
    send[2] = (kept[1 - high] + near[2 - high].astype(F32)).astype(BF16)
    keep[...] = kept[high] + near[1 + high].astype(F32)


def fourth_kernel(
    where, pair, far, keep, gain, a0, a1, a2, a3, grad_n, normed, scale, inner, mids, acts
):
    chip, layer = where[0], where[2]
    mids[layer] = pair[0].astype(F32)
    mids[layer ^ 1] = pair[1].astype(F32)
    mids[layer ^ 2] = far[0].astype(F32)
    mids[layer ^ 3] = far[1].astype(F32)
    squares = sum(mids[j] * mids[j] for j in range(4))
    width = 4 * gain.shape[2]
    root = lax.rsqrt(jnp.sum(squares, axis=-1, keepdims=True) / width + EPS)
    for j in range(4):
        acts[j] = gelu_tanh(mids[j] * root * gain[j]).astype(BF16)
    for step, out in enumerate((a0, a1, a2, a3)):
        out[...] = acts[chip ^ step]
    n = mids[layer] * root
    g = gain[layer]
    back = keep[...] + far[2].astype(F32)
    grad = back * gelu_slope(n * g) * g
    grad_n[...] = grad
    normed[...] = n
    scale[...] = jnp.broadcast_to(root, scale.shape)
    inner[...] = jnp.broadcast_to(jnp.sum(grad * n, axis=-1, keepdims=True), inner.shape)


def fifth_kernel(where, a0, a1, a2, a3, grad_n, normed, scale, i0, i1, t0, t1, t2, t3, *, width):
    inner = (i0[:, 0:1] + i1[:, 0:1]) * (1.0 / width)
    grad = (scale[:, 0:1] * (grad_n[...] - normed[...] * inner)).astype(BF16)
    for a, t in ((a0, t0), (a1, t1), (a2, t2), (a3, t3)):
        t[0] = a[...]
        t[1] = grad


def sixth_kernel(where, t0, t1, t2, t3, wa, wa_o, send, kept, rows, whole_a, total):
    chip, core, low = where[0], where[1], where[2] % 2
    block = t0.shape[1] // 2
    length = 4 * block
    join_cores(whole_a, wa, wa_o, core)
    for step, t in enumerate((t0, t1, t2, t3)):
        at = pl.multiple_of(block * (chip ^ step), 32)
        for half in range(2):
            rows[pl.ds(pl.multiple_of(length * half + at, 32), block), :] = t[
                1, block * half : block * half + block, :
            ]
    u = rows[...]
    p = [dot_t(u, whole_a[t]) for t in range(5)]
    e = [v[0:length] for v in p]
    o = [v[length : 2 * length] for v in p]
    total[0] = 0.5 * (o[0] + e[1] + e[2] + earlier(o[3] + o[4]))
    total[1] = 0.5 * (o[0] + o[1] + e[2] + e[3] + earlier(o[4]))
    total[2] = 0.5 * (later(e[0]) + o[1] + o[2] + e[3] + e[4])
    total[3] = 0.5 * (later(e[0] + e[1]) + o[2] + o[3] + e[4])
    for high in range(2):
        away = pl.multiple_of(block * (2 * high + 1 - low), 32)
        here = pl.multiple_of(block * (2 * high + low), 32)
        for plane in range(4):
            at = slice(block * plane, block * plane + block)
            send[high, at, :] = total[plane, pl.ds(away, block), :].astype(BF16)
            kept[high, at, :] = total[plane, pl.ds(here, block), :]


def out_kernel(where, t0, t1, t2, t3, wb, wb_o, own, s1, s2, s3, rows, whole_b, total):
    chip, core = where[0], where[1]
    block = t0.shape[1] // 2
    join_cores(whole_b, wb, wb_o, core)
    for step, t in enumerate((t0, t1, t2, t3)):
        at = pl.multiple_of(block * (chip ^ step), 32)
        for half in range(2):
            rows[half, pl.ds(at, block), :] = t[0, block * half : block * half + block, :].astype(F32)
    even, odd = rows[0], rows[1]
    qe = 0.5 * (even + odd)
    qo = 0.5 * (odd + later(even))
    qo_early = 0.5 * (earlier(odd) + even)
    cols = (earlier(qe), qo_early, qe, qo, later(qe))
    acc = dot(cols[0].astype(BF16), whole_b[0])
    for t in range(1, 5):
        acc = acc + dot(cols[t].astype(BF16), whole_b[t])
    total[...] = acc
    for step, out in enumerate((own, s1, s2, s3)):
        at = pl.multiple_of(block * (chip ^ step), 32)
        out[...] = total[pl.ds(at, block), :].astype(out.dtype)


def add_out_kernel(where, own, r1, r2, r3, bias, mine, send, total):
    core = where[1]
    part = own.shape[0] // 2
    value = own[...] + r1[...].astype(F32) + r2[...].astype(F32) + r3[...].astype(F32)
    total[...] = (value + bias[...]).astype(BF16)
    mine[...] = total[pl.ds(pl.multiple_of(part * core, 16), part), :]
    send[...] = total[pl.ds(pl.multiple_of(part * (1 - core), 16), part), :]


def put_out_kernel(where, mine, other, out):
    core = where[1]
    out[core] = mine[...]
    out[1 - core] = other[...]


def seventh_kernel(where, kept, near, send, keep):
    high = where[2] // 2
    send[...] = (kept[1 - high] + near[1 - high].astype(F32)).astype(BF16)
    keep[...] = kept[high] + near[high].astype(F32)


def eighth_kernel(where, keep, far, b0, b1, b2, b3, gain, grad_n, normed, inner):
    chip, layer = where[0], where[2]
    rows, share = keep.shape
    step = chip ^ layer
    low = jnp.where(step == 0, b0[0:rows, 0:share], b1[0:rows, 0:share])
    high = jnp.where(step == 2, b2[0:rows, 0:share], b3[0:rows, 0:share])
    n = jnp.where(step < 2, low, high).astype(F32)
    g = gain[chip]
    back = keep[...] + far[...].astype(F32)
    grad = back * gelu_slope(n * g) * g
    grad_n[...] = grad
    normed[...] = n
    inner[...] = jnp.broadcast_to(jnp.sum(grad * n, axis=-1, keepdims=True), inner.shape)


def ninth_kernel(where, grad_n, normed, i0, i1, same, cross, *, width):
    core = where[1]
    block = grad_n.shape[0] // 4
    part = block // 2
    inner = (i0[:, 0:1] + i1[:, 0:1]) * (1.0 / width)
    grad = grad_n[...] - normed[...] * inner
    for plane in range(4):
        at = slice(part * plane, part * plane + part)
        lower = grad[block * plane : block * plane + part].astype(BF16)
        upper = grad[block * plane + part : block * plane + block].astype(BF16)
        same[at, :] = jnp.where(core == 0, lower, upper)
        cross[at, :] = jnp.where(core == 0, upper, lower)


def last_kernel(where, same, cross, dna, out, rows):
    core = where[1]
    part = dna.shape[1] // 4
    for x, window in ((same, core), (cross, 1 - core)):
        v = dna[window].astype(F32)
        root = lax.rsqrt(jnp.mean(v * v, axis=-1, keepdims=True) + EPS)
        share = x.shape[1]
        for plane in range(4):
            taken = x[part * plane : part * plane + part, :].astype(F32)
            for tile in range(rows.shape[0]):
                lanes = min(128, share - 128 * tile)
                rows[tile, pl.ds(plane, part, stride=4), 0:lanes] = taken[
                    :, 128 * tile : 128 * tile + lanes
                ]
        whole = jnp.concatenate([rows[tile] for tile in range(rows.shape[0])], axis=1)
        out[window] = (whole[:, 0:share] * root).astype(BF16)


def stationary(dna_features, gain_a, conv_a, bias_a, gain_b, conv_b, bias_b, grad_out):
    chips = lax.axis_size("ch")
    place = lax.axis_index("seq")
    layer = lax.axis_index("ch")
    chip, core = place // 2, place % 2
    where = jnp.stack([chip, core, layer]).astype(jnp.int32)
    windows, rows_in, width_in = dna_features.shape
    width_mid = gain_b.shape[0]
    share_in, share_mid, share_out = width_in // chips, bias_a.shape[0], bias_b.shape[0]
    part = rows_in // 4
    block = 2 * part
    length = chips * block
    taps = conv_a.shape[0]
    gain_in = gain_a.reshape(chips, 1, share_in)
    gain_mid = gain_b.reshape(chips, 1, share_mid)
    steps = range(1, chips)

    dna_other = swap(lax.dynamic_index_in_dim(dna_features, 1 - core, 0, False), "seq", 1)
    cot_other = swap(lax.dynamic_index_in_dim(grad_out, 1 - core, 0, False), "seq", 1)
    other_a = swap(conv_a, "seq", 1)
    other_b = swap(conv_b, "seq", 1)

    packed = ((5 * block, share_out), BF16)
    blocks = call(
        pack_kernel,
        [packed] * 4,
        where,
        (dna_features, dna_other, grad_out, cot_other),
        [((width_in // 128, rows_in, 128), F32), ((chips, 4 * block, share_in), BF16)],
    )
    blocks = [blocks[0]] + [swap(blocks[d], "seq", 2 * d) for d in steps]

    pair = (2, 2 * block, share_mid)
    sums = call(
        first_kernel,
        [(pair, F32)] + [(pair, BF16)] * 3,
        where,
        (*blocks, gain_in, conv_a, other_a, conv_b, other_b),
        [
            ((4, length, share_in), BF16),
            ((length, share_out), BF16),
            ((taps, 2 * length, share_in), BF16),
            ((taps, share_in, share_mid), BF16),
            ((taps, share_mid, share_out), BF16),
            ((4, length, share_mid), F32),
        ],
    )
    sums = [sums[0]] + [swap(sums[d], "seq", 2 * d) for d in steps]
    one = (2 * block, share_mid)
    mid, send, kept = call(
        second_kernel,
        [(one, BF16), ((3,) + one, BF16), ((2,) + one, F32)],
        where,
        (*sums, bias_a.reshape(1, share_mid)),
        [((chips,) + one, F32)],
    )
    near = swap(send, "ch", 1)
    pair_mid, keep = call(
        third_kernel, [((3,) + one, BF16), (one, F32)], where, (mid, near, kept)
    )
    far = swap(pair_mid, "ch", 2)
    lane = (2 * block, 128)
    *acts, grad_n, normed, scale, inner = call(
        fourth_kernel,
        [(one, BF16)] * 4 + [(one, F32), (one, F32), (lane, F32), (lane, F32)],
        where,
        (pair_mid, far, keep, gain_mid),
        [((chips,) + one, F32), ((chips,) + one, BF16)],
    )
    inner = inner + swap(inner, "ch", 1)
    inner_far = swap(inner, "ch", 2)
    rest = call(
        functools.partial(fifth_kernel, width=width_mid),
        [(pair, BF16)] * 4,
        where,
        (*acts, grad_n, normed, scale, inner, inner_far),
    )
    rest = [rest[0]] + [swap(rest[d], "seq", 2 * d) for d in steps]

    quarter = (4 * block, share_in)
    send, kept = call(
        sixth_kernel,
        [((2,) + quarter, BF16), ((2,) + quarter, F32)],
        where,
        (*rest, conv_a, other_a),
        [
            ((2 * length, share_mid), BF16),
            ((taps, share_in, share_mid), BF16),
            ((4, length, share_in), F32),
        ],
    )
    near = swap(send, "ch", 1)
    outs = call(
        out_kernel,
        [((block, share_out), F32)] + [((block, share_out), BF16)] * 3,
        where,
        (*rest, conv_b, other_b),
        [
            ((2, length, share_mid), F32),
            ((taps, share_mid, share_out), BF16),
            ((length, share_out), F32),
        ],
    )
    outs, near = lax.optimization_barrier((outs, near))
    send, keep = call(seventh_kernel, [(quarter, BF16), (quarter, F32)], where, (kept, near))
    far = swap(send, "ch", 2)
    outs = [outs[0]] + [swap(outs[d], "seq", 2 * d) for d in steps]
    lane = (4 * block, 128)
    grad_n, normed, inner = call(
        eighth_kernel,
        [(quarter, F32), (quarter, F32), (lane, F32)],
        where,
        (keep, far, *blocks, gain_in),
    )
    inner = inner + swap(inner, "seq", 2)
    inner_far = swap(inner, "seq", 4)
    same, cross = call(
        functools.partial(ninth_kernel, width=width_in),
        [((4 * part, share_in), BF16)] * 2,
        where,
        (grad_n, normed, inner, inner_far),
    )
    same, cross = transpose_chips(same, 0), transpose_chips(cross, 1)

    mine, send = call(
        add_out_kernel,
        [((part, share_out), BF16)] * 2,
        where,
        (*outs, bias_b.reshape(1, share_out)),
        [((block, share_out), BF16)],
    )
    other = swap(send, "seq", 1)
    (pooled_out,) = call(
        put_out_kernel, [(grad_out.shape, BF16)], where, (mine, other)
    )
    (input_grad,) = call(
        last_kernel,
        [((windows, rows_in, share_in), BF16)],
        where,
        (same, cross, dna_features),
        [((-(-share_in // 128), rows_in, 128), F32)],
    )
    return (pooled_out, input_grad)


def fits(mesh_shape, args):
    places, layers = mesh_shape["seq"], mesh_shape["ch"]
    windows, rows = args[0].shape[0], args[0].shape[1]
    return places == 2 * layers and layers == 4 and windows == 2 and rows == 64 * places


def solution(mesh):
    in_specs = (
        P(None, "seq", None),
        P(),
        P(None, "seq", "ch"),
        P("ch"),
        P(),
        P(None, "seq", "ch"),
        P("ch"),
        P(None, "seq", "ch"),
    )
    out_specs = (P(None, "seq", "ch"), P(None, "seq", "ch"))
    def run(*args):
        plan = stationary if fits(mesh.shape, args) else per_device
        return jax.shard_map(
            plan, mesh=mesh, in_specs=in_specs, out_specs=out_specs, check_vma=False
        )(*args)

    return run
```

```python
import functools
import math

import jax
import jax.numpy as jnp
from jax import lax
from jax.experimental import pallas as pl
from jax.experimental.pallas import tpu as pltpu
from jax.sharding import PartitionSpec as P

EPS = 1e-06
F32, BF16 = jnp.float32, jnp.bfloat16
ROOT = math.sqrt(2.0 / math.pi)


def with_halo(block, sides, width):
    for axis, dim in sides:
        count = lax.axis_size(axis)
        forward = [(i, i + 1) for i in range(count - 1)]
        backward = [(target, source) for source, target in forward]
        low = lax.ppermute(
            lax.slice_in_dim(block, block.shape[dim] - width, None, axis=dim), axis, forward
        )
        high = lax.ppermute(lax.slice_in_dim(block, 0, width, axis=dim), axis, backward)
        block = jnp.concatenate([low, block, high], axis=dim)
    return block


def gelu_tanh(z):
    return 0.5 * z * (1.0 + jnp.tanh(ROOT * (z + 0.044715 * z * z * z)))


def gelu_slope(z):
    t = jnp.tanh(ROOT * (z + 0.044715 * z * z * z))
    return 0.5 * (1.0 + t) + 0.5 * z * (1.0 - t * t) * ROOT * (1.0 + 3.0 * 0.044715 * z * z)


def pool_pairs(v):
    return v.reshape(v.shape[0], v.shape[1] // 2, 2, v.shape[2]).sum(axis=2) * 0.5


def repeat_half(v):
    return (jnp.repeat(v.astype(jnp.float32), 2, axis=1) * 0.5).astype(jnp.bfloat16)


def conv_rows(padded, weight, length):
    total = jnp.einsum(
        "wtc,co->wto", padded[:, 0:length], weight[0], preferred_element_type=jnp.float32
    )
    for offset in range(1, weight.shape[0]):
        total = total + jnp.einsum(
            "wtc,co->wto",
            padded[:, offset : offset + length],
            weight[offset],
            preferred_element_type=jnp.float32,
        )
    return total


def conv_back(padded, weight, length):
    total = jnp.einsum(
        "wto,co->wtc", padded[:, 4 : 4 + length], weight[0], preferred_element_type=jnp.float32
    )
    for offset in range(1, weight.shape[0]):
        start = 4 - offset
        total = total + jnp.einsum(
            "wto,co->wtc",
            padded[:, start : start + length],
            weight[offset],
            preferred_element_type=jnp.float32,
        )
    return total


def per_device(dna_features, gain_a, conv_a, bias_a, gain_b, conv_b, bias_b, grad_out):
    rows_in = dna_features.shape[1]
    rows_mid = rows_in // 2
    width_in = dna_features.shape[2]
    width_mid = gain_b.shape[0]
    share_mid = bias_a.shape[0]
    share_in = width_in // lax.axis_size("ch")
    ch_index = lax.axis_index("ch")
    whole_a, whole_b = (
        lax.all_gather(conv_a, "seq", axis=1, tiled=True),
        lax.all_gather(conv_b, "seq", axis=1, tiled=True),
    )
    feat = dna_features.astype(jnp.float32)
    scale_a = lax.rsqrt(jnp.mean(feat * feat, axis=-1, keepdims=True) + EPS)
    act_a = gelu_tanh(feat * scale_a * gain_a).astype(jnp.bfloat16)
    padded_a = with_halo(act_a, (("seq", 1),), 2)
    conv_out_a = conv_rows(padded_a, whole_a, rows_in)
    mid = pool_pairs(conv_out_a + bias_a).astype(jnp.bfloat16)
    gain_part = lax.dynamic_slice_in_dim(gain_b, ch_index * share_mid, share_mid, 0)
    mid_f = mid.astype(jnp.float32)
    squares = lax.psum(jnp.sum(mid_f * mid_f, axis=-1, keepdims=True), "ch")
    scale_b = lax.rsqrt(squares / width_mid + EPS)
    act_part = gelu_tanh(mid_f * scale_b * gain_part).astype(jnp.bfloat16)
    act_full = lax.all_gather(act_part, "ch", axis=2, tiled=True)
    padded_b = with_halo(act_full, (("seq", 1),), 2)
    conv_out_b = conv_rows(padded_b, whole_b, rows_mid)
    pooled_out = pool_pairs(conv_out_b + bias_b).astype(jnp.bfloat16)
    grad_b = repeat_half(grad_out)
    grad_pad_b = with_halo(grad_b, (("seq", 1),), 2)
    partial_b = conv_back(grad_pad_b, whole_b, rows_mid)
    back_share = lax.psum_scatter(
        partial_b.astype(jnp.bfloat16), "ch", scatter_dimension=2, tiled=True
    ).astype(jnp.float32)
    normed_b = mid_f * scale_b
    grad_n = back_share * gelu_slope(normed_b * gain_part) * gain_part
    inner_b = lax.psum(jnp.sum(grad_n * normed_b, axis=-1, keepdims=True), "ch") / width_mid
    grad_mid = (scale_b * (grad_n - normed_b * inner_b)).astype(jnp.bfloat16)
    grad_a = repeat_half(grad_mid)
    grad_pad_a = with_halo(grad_a, (("seq", 1),), 2)
    partial_a = conv_back(grad_pad_a, whole_a, rows_in)
    back_share_a = lax.psum_scatter(
        partial_a.astype(jnp.bfloat16), "ch", scatter_dimension=2, tiled=True
    ).astype(jnp.float32)
    feat_part = lax.dynamic_slice_in_dim(feat, ch_index * share_in, share_in, 2)
    gain_part_a = lax.dynamic_slice_in_dim(gain_a, ch_index * share_in, share_in, 0)
    normed_a = feat_part * scale_a
    grad_na = back_share_a * gelu_slope(normed_a * gain_part_a) * gain_part_a
    inner_a = lax.psum(jnp.sum(grad_na * normed_a, axis=-1, keepdims=True), "ch") / width_in
    input_grad = (scale_a * (grad_na - normed_a * inner_a)).astype(jnp.bfloat16)
    return (pooled_out, input_grad)


def swap(x, axis, bit):
    count = lax.axis_size(axis)
    return lax.ppermute(x, axis, [(i, i ^ bit) for i in range(count)])


def transpose_chips(x, flip):
    chips = lax.axis_size("ch")
    pairs = []
    for chip in range(chips):
        for core in range(2):
            for layer in range(chips):
                source = (2 * chip + core) * chips + layer
                pairs.append((source, (2 * layer + (core ^ flip)) * chips + chip))
    return lax.ppermute(x, ("seq", "ch"), pairs)


def call(body, outs, where, operands, scratch=(), flops=0, grant=16 << 20):
    total = sum(math.prod(s) * jnp.dtype(t).itemsize for s, t in outs)
    total += sum(a.size * a.dtype.itemsize for a in operands)
    return pl.pallas_call(
        body,
        out_shape=[jax.ShapeDtypeStruct(s, t) for s, t in outs],
        in_specs=[pl.BlockSpec(memory_space=pltpu.SMEM)]
        + [pl.BlockSpec(memory_space=pltpu.VMEM)] * len(operands),
        out_specs=[pl.BlockSpec(memory_space=pltpu.VMEM)] * len(outs),
        scratch_shapes=[pltpu.VMEM(s, t) for s, t in scratch],
        compiler_params=pltpu.CompilerParams(vmem_limit_bytes=grant),
        cost_estimate=pl.CostEstimate(flops=flops, bytes_accessed=total, transcendentals=0),
    )(where, *operands)


def later(v):
    rows = lax.broadcasted_iota(jnp.int32, v.shape, 0)
    return jnp.where(rows == v.shape[0] - 1, 0.0, pltpu.roll(v, v.shape[0] - 1, 0))


def earlier(v):
    rows = lax.broadcasted_iota(jnp.int32, v.shape, 0)
    return jnp.where(rows == 0, 0.0, pltpu.roll(v, 1, 0))


def dot(a, b):
    return jnp.dot(a, b, preferred_element_type=F32)


def dot_t(a, b):
    return lax.dot_general(a, b, (((1,), (1,)), ((), ())), preferred_element_type=F32)


def join_cores(whole, mine, other, core):
    half = mine.shape[1]
    for t in range(mine.shape[0]):
        whole[t, pl.ds(pl.multiple_of(core * half, 16), half), :] = mine[t]
        whole[t, pl.ds(pl.multiple_of((1 - core) * half, 16), half), :] = other[t]


def join_kernel(where, wa, wa_o, wb, wb_o, whole_a, whole_b):
    join_cores(whole_a, wa, wa_o, where[1])
    join_cores(whole_b, wb, wb_o, where[1])


def start_kernel(where, dna, cot, keep, send, rows):
    core = where[1]
    part = dna.shape[1] // 4
    width = cot.shape[2]
    tiles = rows.shape[0]
    for out, window in ((send, 1 - core), (keep, core)):
        v = dna[window].astype(F32)
        v = v * lax.rsqrt(jnp.mean(v * v, axis=-1, keepdims=True) + EPS)
        for tile in range(tiles):
            rows[tile] = v[:, 128 * tile : 128 * tile + 128]
        for plane in range(4):
            taken = [rows[tile, pl.ds(plane, part, stride=4), :] for tile in range(tiles)]
            taken = jnp.concatenate(taken, axis=1).astype(BF16)
            out[part * plane : part * plane + part, :] = taken
        out[4 * part :, 0:width] = cot[window]


def split_share(share):
    return share * 4 // 5, share // 5


def pack_kernel(where, keep, other, b0, b1, b2, b3, shares, cots):
    chip, core = where[0], where[1]
    part = keep.shape[0] // 5
    share = keep.shape[1] // 4
    width = cots.shape[1]
    main, tail = split_share(share)
    for source, position in ((keep, core), (other, 1 - core)):
        for plane in range(4):
            at = pl.multiple_of(2 * part * plane + part * position, 16)
            for j in range(4):
                shares[j, pl.ds(at, part), :] = source[
                    part * plane : part * plane + part, share * j : share * j + share
                ]
        cots[pl.ds(pl.multiple_of(part * position, 16), part), :] = source[4 * part :, 0:width]
    block = 2 * part
    rest = width - main
    for step, out in enumerate((b0, b1, b2, b3)):
        rows = shares[chip ^ step]
        out[0 : 4 * block, :] = rows[:, 0:main]
        tails = [rows[block * plane : block * plane + block, main:share] for plane in range(4)]
        out[4 * block : 5 * block, :] = jnp.concatenate(tails, axis=1)
        out[5 * block : 6 * block, :] = cots[:, 0:main]
        out[6 * block :, 0:rest] = cots[0:part, main:width]
        out[6 * block :, rest : 2 * rest] = cots[part:block, main:width]


def open_plane(packed, plane, rows, tail):
    return jnp.concatenate(
        [
            packed[rows * plane : rows * plane + rows, :],
            packed[4 * rows : 5 * rows, tail * plane : tail * plane + tail],
        ],
        axis=1,
    )


def over_tails(column, rows, tail):
    parts = [column[rows * plane : rows * plane + rows] for plane in range(4)]
    parts = [jnp.broadcast_to(v, (rows, tail)) for v in parts]
    return jnp.concatenate(parts, axis=1)


def to_row(column):
    wide = jnp.broadcast_to(column, (column.shape[0], 128))
    if column.shape[0] < 128:
        wide = jnp.concatenate([wide, jnp.zeros((128 - column.shape[0], 128), F32)], axis=0)
    return jnp.transpose(wide)[0:8, :]


def to_column(row, rows):
    wide = jnp.concatenate([row] * 16, axis=0)
    return jnp.transpose(wide)[0:rows, 0:1]


def first_kernel(
    where, b0, b1, b2, b3, gain, whole_a, whole_b,
    own, s1, s2, s3, planes, cots, cols, total,
):
    chip = where[0]
    block = planes.shape[1] // 4
    part = block // 2
    share = gain.shape[2]
    main, tail = split_share(share)
    rest = cots.shape[1] - main
    for step, b in enumerate((b0, b1, b2, b3)):
        at = pl.multiple_of(block * (chip ^ step), 32)
        for plane in range(4):
            planes[plane, pl.ds(at, block), :] = open_plane(b, plane, block, tail)
        cots[pl.ds(at, block), 0:main] = b[5 * block : 6 * block, :]
        low = pl.multiple_of(at + part, 16)
        cots[pl.ds(at, part), main:] = b[6 * block :, 0:rest]
        cots[pl.ds(low, part), main:] = b[6 * block :, rest : 2 * rest]
    length = 4 * block
    g = gain[chip]
    act = [gelu_tanh(planes[plane].astype(F32) * g) for plane in range(4)]
    pa = 0.5 * (act[0] + act[1])
    pb = 0.5 * (act[1] + act[2])
    pc = 0.5 * (act[2] + act[3])
    pd = 0.5 * (act[3] + later(act[0]))
    pd_early = 0.5 * (earlier(act[3]) + act[0])
    even = (earlier(pc), pd_early, pa, pb, pc)
    odd = (pa, pb, pc, pd, later(pa))
    for t in range(5):
        cols[t, 0:length, :] = even[t].astype(BF16)
        cols[t, length : 2 * length, :] = odd[t].astype(BF16)
    acc = dot(cols[0], whole_a[0])
    for t in range(1, 5):
        acc = acc + dot(cols[t], whole_a[t])
    total[0] = acc[0:length]
    total[1] = acc[length : 2 * length]
    c = cots[...]
    p = [dot_t(c, whole_b[t]) for t in range(5)]
    total[2] = 0.5 * (later(p[0]) + p[1] + p[2] + earlier(p[3] + p[4]))
    total[3] = 0.5 * (later(p[0] + p[1]) + p[2] + p[3] + earlier(p[4]))
    for step, out in enumerate((own, s1, s2, s3)):
        at = pl.multiple_of(block * (chip ^ step), 32)
        for kind in range(2):
            for half in range(2):
                out[kind, block * half : block * half + block, :] = total[
                    2 * kind + half, pl.ds(at, block), :
                ].astype(out.dtype)


def second_kernel(where, own, r1, r2, r3, bias, mid, send, kept, back):
    chip, low = where[0], where[2] % 2
    value = own[0] + r1[0].astype(F32) + r2[0].astype(F32) + r3[0].astype(F32) + bias[...]
    mid[...] = value.astype(BF16)
    send[0] = value.astype(BF16)
    back[chip] = own[1]
    for step, r in ((1, r1), (2, r2), (3, r3)):
        back[chip ^ step] = r[1].astype(F32)
    for high in range(2):
        send[1 + high] = back[2 * high + 1 - low].astype(BF16)
        kept[high] = back[2 * high + low]


def third_kernel(where, mid, near, kept, send, keep):
    high = where[2] // 2
    send[0] = mid[...]
    send[1] = near[0]
    send[2] = (kept[1 - high] + near[2 - high].astype(F32)).astype(BF16)
    keep[...] = kept[high] + near[1 + high].astype(F32)


def fourth_kernel(
    where, pair, far, keep, gain, a0, a1, a2, a3, grad_n, normed, scale, inner, mids, acts
):
    chip, layer = where[0], where[2]
    mids[layer] = pair[0].astype(F32)
    mids[layer ^ 1] = pair[1].astype(F32)
    mids[layer ^ 2] = far[0].astype(F32)
    mids[layer ^ 3] = far[1].astype(F32)
    squares = sum(mids[j] * mids[j] for j in range(4))
    width = 4 * gain.shape[2]
    root = lax.rsqrt(jnp.sum(squares, axis=-1, keepdims=True) / width + EPS)
    for j in range(4):
        acts[j] = gelu_tanh(mids[j] * root * gain[j]).astype(BF16)
    for step, out in enumerate((a0, a1, a2, a3)):
        out[...] = acts[chip ^ step]
    n = mids[layer] * root
    g = gain[layer]
    back = keep[...] + far[2].astype(F32)
    grad = back * gelu_slope(n * g) * g
    grad_n[...] = grad
    normed[...] = n
    scale[...] = jnp.broadcast_to(root, scale.shape)
    inner[...] = to_row(jnp.sum(grad * n, axis=-1, keepdims=True))


def fifth_kernel(where, a0, a1, a2, a3, grad_n, normed, scale, i0, i1, t0, t1, t2, t3, *, width):
    inner = to_column(i0[...] + i1[...], grad_n.shape[0]) * (1.0 / width)
    grad = (scale[:, 0:1] * (grad_n[...] - normed[...] * inner)).astype(BF16)
    for a, t in ((a0, t0), (a1, t1), (a2, t2), (a3, t3)):
        t[0] = a[...]
        t[1] = grad


def sixth_kernel(where, t0, t1, t2, t3, whole_a, send, kept, rows, total):
    chip, low = where[0], where[2] % 2
    block = t0.shape[1] // 2
    length = 4 * block
    share = whole_a.shape[1]
    main, tail = split_share(share)
    for step, t in enumerate((t0, t1, t2, t3)):
        at = pl.multiple_of(block * (chip ^ step), 32)
        for half in range(2):
            rows[pl.ds(pl.multiple_of(length * half + at, 32), block), :] = t[
                1, block * half : block * half + block, :
            ]
    u = rows[...]
    p = [dot_t(u, whole_a[t]) for t in range(5)]
    e = [v[0:length] for v in p]
    o = [v[length : 2 * length] for v in p]
    total[0] = 0.5 * (o[0] + e[1] + e[2] + earlier(o[3] + o[4]))
    total[1] = 0.5 * (o[0] + o[1] + e[2] + e[3] + earlier(o[4]))
    total[2] = 0.5 * (later(e[0]) + o[1] + o[2] + e[3] + e[4])
    total[3] = 0.5 * (later(e[0] + e[1]) + o[2] + o[3] + e[4])
    for high in range(2):
        away = pl.multiple_of(block * (2 * high + 1 - low), 32)
        here = pl.multiple_of(block * (2 * high + low), 32)
        for out, start in ((send, away), (kept, here)):
            tails = []
            for plane in range(4):
                taken = total[plane, pl.ds(start, block), :]
                out[high, block * plane : block * plane + block, :] = taken[:, 0:main].astype(out.dtype)
                tails.append(taken[:, main:share])
            out[high, 4 * block : 5 * block, :] = jnp.concatenate(tails, axis=1).astype(out.dtype)


def out_kernel(where, t0, t1, t2, t3, whole_b, own, s1, s2, s3, rows, total):
    chip = where[0]
    block = t0.shape[1] // 2
    for step, t in enumerate((t0, t1, t2, t3)):
        at = pl.multiple_of(block * (chip ^ step), 32)
        for half in range(2):
            rows[half, pl.ds(at, block), :] = t[0, block * half : block * half + block, :].astype(F32)
    even, odd = rows[0], rows[1]
    qe = 0.5 * (even + odd)
    qo = 0.5 * (odd + later(even))
    qo_early = 0.5 * (earlier(odd) + even)
    cols = (earlier(qe), qo_early, qe, qo, later(qe))
    acc = dot(cols[0].astype(BF16), whole_b[0])
    for t in range(1, 5):
        acc = acc + dot(cols[t].astype(BF16), whole_b[t])
    total[...] = acc
    for step, out in enumerate((own, s1, s2, s3)):
        at = pl.multiple_of(block * (chip ^ step), 32)
        out[...] = total[pl.ds(at, block), :].astype(out.dtype)


def add_out_kernel(where, own, r1, r2, r3, bias, mine, send, total):
    core = where[1]
    part = own.shape[0] // 2
    value = own[...] + r1[...].astype(F32) + r2[...].astype(F32) + r3[...].astype(F32)
    total[...] = (value + bias[...]).astype(BF16)
    mine[...] = total[pl.ds(pl.multiple_of(part * core, 16), part), :]
    send[...] = total[pl.ds(pl.multiple_of(part * (1 - core), 16), part), :]


def put_out_kernel(where, mine, other, out):
    core = where[1]
    out[core] = mine[...]
    out[1 - core] = other[...]


def seventh_kernel(where, kept, near, send, keep):
    high = where[2] // 2
    send[...] = (kept[1 - high] + near[1 - high].astype(F32)).astype(BF16)
    keep[...] = kept[high] + near[high].astype(F32)


def eighth_kernel(where, keep, far, b0, b1, b2, b3, gain, grad_n, normed, inner):
    chip, layer = where[0], where[2]
    rows, main = keep.shape
    block = rows // 5
    tail = main // 4
    step = chip ^ layer
    low = jnp.where(step == 0, b0[0:rows], b1[0:rows])
    high = jnp.where(step == 2, b2[0:rows], b3[0:rows])
    n = jnp.where(step < 2, low, high).astype(F32)
    g = gain[chip]
    back = keep[...] + far[...].astype(F32)
    sides = ((0, 4 * block, g[:, 0:main]), (4 * block, rows, jnp.concatenate([g[:, main:]] * 4, axis=1)))
    products = []
    for start, stop, weight in sides:
        part = n[start:stop]
        grad = back[start:stop] * gelu_slope(part * weight) * weight
        grad_n[start:stop, :] = grad
        products.append(grad * part)
    normed[...] = n
    column = jnp.sum(products[0], axis=-1, keepdims=True)
    tails = [
        jnp.sum(products[1][:, tail * plane : tail * plane + tail], axis=-1, keepdims=True)
        for plane in range(4)
    ]
    inner[...] = to_row(column + jnp.concatenate(tails, axis=0))


def ninth_kernel(where, grad_n, normed, i0, i1, i2, i3, same, cross, total, *, width):
    core = where[1]
    rows, main = grad_n.shape
    block = rows // 5
    part = block // 2
    tail = main // 4
    inner = to_column(i0[...] + i1[...] + i2[...] + i3[...], 4 * block) * (1.0 / width)
    top = slice(0, 4 * block)
    low = slice(4 * block, rows)
    total[top, :] = grad_n[top, :] - normed[top, :] * inner
    total[low, :] = grad_n[low, :] - normed[low, :] * over_tails(inner, block, tail)
    for plane in range(5):
        at = slice(part * plane, part * plane + part)
        lower = total[block * plane : block * plane + part, :].astype(BF16)
        upper = total[block * plane + part : block * plane + block, :].astype(BF16)
        same[at, :] = jnp.where(core == 0, lower, upper)
        cross[at, :] = jnp.where(core == 0, upper, lower)


def last_kernel(where, same, cross, dna, out, rows):
    core = where[1]
    part = dna.shape[1] // 4
    share = out.shape[2]
    main, tail = split_share(share)
    for x, window in ((same, core), (cross, 1 - core)):
        v = dna[window].astype(F32)
        root = lax.rsqrt(jnp.mean(v * v, axis=-1, keepdims=True) + EPS)
        for plane in range(4):
            taken = open_plane(x, plane, part, tail).astype(F32)
            for tile in range(rows.shape[0]):
                lanes = min(128, share - 128 * tile)
                rows[tile, pl.ds(plane, part, stride=4), 0:lanes] = taken[
                    :, 128 * tile : 128 * tile + lanes
                ]
        whole = jnp.concatenate([rows[tile] for tile in range(rows.shape[0])], axis=1)
        out[window] = (whole[:, 0:share] * root).astype(BF16)


def stationary(dna_features, gain_a, conv_a, bias_a, gain_b, conv_b, bias_b, grad_out):
    chips = lax.axis_size("ch")
    place = lax.axis_index("seq")
    layer = lax.axis_index("ch")
    chip, core = place // 2, place % 2
    where = jnp.stack([chip, core, layer]).astype(jnp.int32)
    windows, rows_in, width_in = dna_features.shape
    width_mid = gain_b.shape[0]
    share_in, share_mid, share_out = width_in // chips, bias_a.shape[0], bias_b.shape[0]
    part = rows_in // 4
    block = 2 * part
    length = chips * block
    taps = conv_a.shape[0]
    gain_in = gain_a.reshape(chips, 1, share_in)
    gain_mid = gain_b.reshape(chips, 1, share_mid)
    steps = range(1, chips)

    other_a = swap(conv_a, "seq", 1)
    other_b = swap(conv_b, "seq", 1)
    half = ((5 * part, width_in), BF16)
    keep, send = call(
        start_kernel,
        [half] * 2,
        where,
        (dna_features, grad_out),
        [((width_in // 128, rows_in, 128), F32)],
    )
    other = swap(send, "seq", 1)
    main, tail = split_share(share_in)
    packed = ((13 * part, main), BF16)
    blocks = call(
        pack_kernel,
        [packed] * 4,
        where,
        (keep, other),
        [((chips, 4 * block, share_in), BF16), ((block, share_out), BF16)],
    )
    *blocks, conv_a, other_a, conv_b, other_b = lax.optimization_barrier(
        (*blocks, conv_a, other_a, conv_b, other_b)
    )
    whole_a, whole_b = call(
        join_kernel,
        [((taps, share_in, share_mid), BF16), ((taps, share_mid, share_out), BF16)],
        where,
        (conv_a, other_a, conv_b, other_b),
    )
    blocks = [blocks[0]] + [swap(blocks[d], "seq", 2 * d) for d in steps]

    pair = (2, 2 * block, share_mid)
    sums = call(
        first_kernel,
        [(pair, F32)] + [(pair, BF16)] * 3,
        where,
        (*blocks, gain_in, whole_a, whole_b),
        [
            ((4, length, share_in), BF16),
            ((length, share_out), BF16),
            ((taps, 2 * length, share_in), BF16),
            ((4, length, share_mid), F32),
        ],
    )
    sums = [sums[0]] + [swap(sums[d], "seq", 2 * d) for d in steps]
    one = (2 * block, share_mid)
    mid, send, kept = call(
        second_kernel,
        [(one, BF16), ((3,) + one, BF16), ((2,) + one, F32)],
        where,
        (*sums, bias_a.reshape(1, share_mid)),
        [((chips,) + one, F32)],
    )
    near = swap(send, "ch", 1)
    pair_mid, keep = call(
        third_kernel, [((3,) + one, BF16), (one, F32)], where, (mid, near, kept)
    )
    far = swap(pair_mid, "ch", 2)
    lane = (2 * block, 128)
    row = (8, 128)
    *acts, grad_n, normed, scale, inner = call(
        fourth_kernel,
        [(one, BF16)] * 4 + [(one, F32), (one, F32), (lane, F32), (row, F32)],
        where,
        (pair_mid, far, keep, gain_mid),
        [((chips,) + one, F32), ((chips,) + one, BF16)],
    )
    inner = inner + swap(inner, "ch", 1)
    inner_far = swap(inner, "ch", 2)
    rest = call(
        functools.partial(fifth_kernel, width=width_mid),
        [(pair, BF16)] * 4,
        where,
        (*acts, grad_n, normed, scale, inner, inner_far),
    )
    rest = [rest[0]] + [swap(rest[d], "seq", 2 * d) for d in steps]

    quarter = (5 * block, main)
    send, kept = call(
        sixth_kernel,
        [((2,) + quarter, BF16), ((2,) + quarter, F32)],
        where,
        (*rest, whole_a),
        [
            ((2 * length, share_mid), BF16),
            ((4, length, share_in), F32),
        ],
    )
    near = swap(send, "ch", 1)
    outs = call(
        out_kernel,
        [((block, share_out), F32)] + [((block, share_out), BF16)] * 3,
        where,
        (*rest, whole_b),
        [
            ((2, length, share_mid), F32),
            ((length, share_out), F32),
        ],
    )
    outs, near = lax.optimization_barrier((outs, near))
    send, keep = call(seventh_kernel, [(quarter, BF16), (quarter, F32)], where, (kept, near))
    far = swap(send, "ch", 2)
    outs = [outs[0]] + [swap(outs[d], "seq", 2 * d) for d in steps]
    outs, far = lax.optimization_barrier((outs, far))
    grad_n, normed, inner = call(
        eighth_kernel,
        [(quarter, F32), (quarter, F32), (row, F32)],
        where,
        (keep, far, *blocks, gain_in),
    )
    inners = [inner] + [swap(inner, "seq", 2 * d) for d in steps]
    mine, send = call(
        add_out_kernel,
        [((part, share_out), BF16)] * 2,
        where,
        (*outs, bias_b.reshape(1, share_out)),
        [((block, share_out), BF16)],
    )
    other = swap(send, "seq", 1)
    inners, other = lax.optimization_barrier((inners, other))
    same, cross = call(
        functools.partial(ninth_kernel, width=width_in),
        [((5 * part, main), BF16)] * 2,
        where,
        (grad_n, normed, *inners),
        [(quarter, F32)],
    )
    same, cross = transpose_chips(same, 0), transpose_chips(cross, 1)
    (pooled_out,) = call(
        put_out_kernel, [(grad_out.shape, BF16)], where, (mine, other)
    )
    (input_grad,) = call(
        last_kernel,
        [((windows, rows_in, share_in), BF16)],
        where,
        (same, cross, dna_features),
        [((-(-share_in // 128), rows_in, 128), F32)],
    )
    return (pooled_out, input_grad)


def fits(mesh_shape, args):
    places, layers = mesh_shape["seq"], mesh_shape["ch"]
    windows, rows = args[0].shape[0], args[0].shape[1]
    share_in, share_out = args[0].shape[2] // layers, args[7].shape[2] // layers
    main, tail = split_share(share_in)
    even = main + tail == share_in and main % 256 == 0 and 2 * (share_out - main) == main
    return even and places == 2 * layers and layers == 4 and windows == 2 and rows == 64 * places


def solution(mesh):
    in_specs = (
        P(None, "seq", None),
        P(),
        P(None, "seq", "ch"),
        P("ch"),
        P(),
        P(None, "seq", "ch"),
        P("ch"),
        P(None, "seq", "ch"),
    )
    out_specs = (P(None, "seq", "ch"), P(None, "seq", "ch"))
    def run(*args):
        plan = stationary if fits(mesh.shape, args) else per_device
        return jax.shard_map(
            plan, mesh=mesh, in_specs=in_specs, out_specs=out_specs, check_vma=False
        )(*args)

    return run
```

```python
import functools
import math

import jax
import jax.numpy as jnp
from jax import lax
from jax.experimental import pallas as pl
from jax.experimental.pallas import tpu as pltpu
from jax.sharding import PartitionSpec as P

EPS = 1e-06
F32, BF16 = jnp.float32, jnp.bfloat16
ROOT = math.sqrt(2.0 / math.pi)


def with_halo(block, sides, width):
    for axis, dim in sides:
        count = lax.axis_size(axis)
        forward = [(i, i + 1) for i in range(count - 1)]
        backward = [(target, source) for source, target in forward]
        low = lax.ppermute(
            lax.slice_in_dim(block, block.shape[dim] - width, None, axis=dim), axis, forward
        )
        high = lax.ppermute(lax.slice_in_dim(block, 0, width, axis=dim), axis, backward)
        block = jnp.concatenate([low, block, high], axis=dim)
    return block


def gelu_tanh(z):
    return 0.5 * z * (1.0 + jnp.tanh(ROOT * (z + 0.044715 * z * z * z)))


def gelu_slope(z):
    t = jnp.tanh(ROOT * (z + 0.044715 * z * z * z))
    return 0.5 * (1.0 + t) + 0.5 * z * (1.0 - t * t) * ROOT * (1.0 + 3.0 * 0.044715 * z * z)


def pool_pairs(v):
    return v.reshape(v.shape[0], v.shape[1] // 2, 2, v.shape[2]).sum(axis=2) * 0.5


def repeat_half(v):
    return (jnp.repeat(v.astype(jnp.float32), 2, axis=1) * 0.5).astype(jnp.bfloat16)


def conv_rows(padded, weight, length):
    total = jnp.einsum(
        "wtc,co->wto", padded[:, 0:length], weight[0], preferred_element_type=jnp.float32
    )
    for offset in range(1, weight.shape[0]):
        total = total + jnp.einsum(
            "wtc,co->wto",
            padded[:, offset : offset + length],
            weight[offset],
            preferred_element_type=jnp.float32,
        )
    return total


def conv_back(padded, weight, length):
    total = jnp.einsum(
        "wto,co->wtc", padded[:, 4 : 4 + length], weight[0], preferred_element_type=jnp.float32
    )
    for offset in range(1, weight.shape[0]):
        start = 4 - offset
        total = total + jnp.einsum(
            "wto,co->wtc",
            padded[:, start : start + length],
            weight[offset],
            preferred_element_type=jnp.float32,
        )
    return total


def per_device(dna_features, gain_a, conv_a, bias_a, gain_b, conv_b, bias_b, grad_out):
    rows_in = dna_features.shape[1]
    rows_mid = rows_in // 2
    width_in = dna_features.shape[2]
    width_mid = gain_b.shape[0]
    share_mid = bias_a.shape[0]
    share_in = width_in // lax.axis_size("ch")
    ch_index = lax.axis_index("ch")
    whole_a, whole_b = (
        lax.all_gather(conv_a, "seq", axis=1, tiled=True),
        lax.all_gather(conv_b, "seq", axis=1, tiled=True),
    )
    feat = dna_features.astype(jnp.float32)
    scale_a = lax.rsqrt(jnp.mean(feat * feat, axis=-1, keepdims=True) + EPS)
    act_a = gelu_tanh(feat * scale_a * gain_a).astype(jnp.bfloat16)
    padded_a = with_halo(act_a, (("seq", 1),), 2)
    conv_out_a = conv_rows(padded_a, whole_a, rows_in)
    mid = pool_pairs(conv_out_a + bias_a).astype(jnp.bfloat16)
    gain_part = lax.dynamic_slice_in_dim(gain_b, ch_index * share_mid, share_mid, 0)
    mid_f = mid.astype(jnp.float32)
    squares = lax.psum(jnp.sum(mid_f * mid_f, axis=-1, keepdims=True), "ch")
    scale_b = lax.rsqrt(squares / width_mid + EPS)
    act_part = gelu_tanh(mid_f * scale_b * gain_part).astype(jnp.bfloat16)
    act_full = lax.all_gather(act_part, "ch", axis=2, tiled=True)
    padded_b = with_halo(act_full, (("seq", 1),), 2)
    conv_out_b = conv_rows(padded_b, whole_b, rows_mid)
    pooled_out = pool_pairs(conv_out_b + bias_b).astype(jnp.bfloat16)
    grad_b = repeat_half(grad_out)
    grad_pad_b = with_halo(grad_b, (("seq", 1),), 2)
    partial_b = conv_back(grad_pad_b, whole_b, rows_mid)
    back_share = lax.psum_scatter(
        partial_b.astype(jnp.bfloat16), "ch", scatter_dimension=2, tiled=True
    ).astype(jnp.float32)
    normed_b = mid_f * scale_b
    grad_n = back_share * gelu_slope(normed_b * gain_part) * gain_part
    inner_b = lax.psum(jnp.sum(grad_n * normed_b, axis=-1, keepdims=True), "ch") / width_mid
    grad_mid = (scale_b * (grad_n - normed_b * inner_b)).astype(jnp.bfloat16)
    grad_a = repeat_half(grad_mid)
    grad_pad_a = with_halo(grad_a, (("seq", 1),), 2)
    partial_a = conv_back(grad_pad_a, whole_a, rows_in)
    back_share_a = lax.psum_scatter(
        partial_a.astype(jnp.bfloat16), "ch", scatter_dimension=2, tiled=True
    ).astype(jnp.float32)
    feat_part = lax.dynamic_slice_in_dim(feat, ch_index * share_in, share_in, 2)
    gain_part_a = lax.dynamic_slice_in_dim(gain_a, ch_index * share_in, share_in, 0)
    normed_a = feat_part * scale_a
    grad_na = back_share_a * gelu_slope(normed_a * gain_part_a) * gain_part_a
    inner_a = lax.psum(jnp.sum(grad_na * normed_a, axis=-1, keepdims=True), "ch") / width_in
    input_grad = (scale_a * (grad_na - normed_a * inner_a)).astype(jnp.bfloat16)
    return (pooled_out, input_grad)


def swap(x, axis, bit):
    count = lax.axis_size(axis)
    return lax.ppermute(x, axis, [(i, i ^ bit) for i in range(count)])


def transpose_chips(x, flip):
    chips = lax.axis_size("ch")
    pairs = []
    for chip in range(chips):
        for core in range(2):
            for layer in range(chips):
                source = (2 * chip + core) * chips + layer
                pairs.append((source, (2 * layer + (core ^ flip)) * chips + chip))
    return lax.ppermute(x, ("seq", "ch"), pairs)


def call(body, outs, where, operands, scratch=(), flops=0, grant=16 << 20, place=pltpu.VMEM, after=()):
    inside = len(operands) + 1
    total = sum(math.prod(s) * jnp.dtype(t).itemsize for s, t in outs)
    total += sum(a.size * a.dtype.itemsize for a in operands)

    def run(*refs):
        body(*refs[:inside], *refs[inside + len(after) :])

    return pl.pallas_call(
        run,
        out_shape=[jax.ShapeDtypeStruct(s, t) for s, t in outs],
        in_specs=[pl.BlockSpec(memory_space=pltpu.SMEM)]
        + [pl.BlockSpec(memory_space=place)] * len(operands)
        + [pl.BlockSpec(memory_space=pl.ANY)] * len(after),
        out_specs=[pl.BlockSpec(memory_space=pltpu.VMEM)] * len(outs),
        scratch_shapes=[pltpu.VMEM(*s) if isinstance(s, tuple) else s for s in scratch],
        compiler_params=pltpu.CompilerParams(vmem_limit_bytes=grant),
        cost_estimate=pl.CostEstimate(flops=flops, bytes_accessed=total, transcendentals=0),
    )(where, *operands, *after)


def later(v):
    rows = lax.broadcasted_iota(jnp.int32, v.shape, 0)
    return jnp.where(rows == v.shape[0] - 1, 0.0, pltpu.roll(v, v.shape[0] - 1, 0))


def earlier(v):
    rows = lax.broadcasted_iota(jnp.int32, v.shape, 0)
    return jnp.where(rows == 0, 0.0, pltpu.roll(v, 1, 0))


def dot(a, b):
    return jnp.dot(a, b, preferred_element_type=F32)


def dot_t(a, b):
    return lax.dot_general(a, b, (((1,), (1,)), ((), ())), preferred_element_type=F32)


def join_cores(whole, mine, other, core):
    half = mine.shape[1]
    for t in range(mine.shape[0]):
        whole[t, pl.ds(pl.multiple_of(core * half, 16), half), :] = mine[t]
        whole[t, pl.ds(pl.multiple_of((1 - core) * half, 16), half), :] = other[t]


def join_kernel(where, wa, wa_o, wb, wb_o, whole_a, whole_b):
    join_cores(whole_a, wa, wa_o, where[1])
    join_cores(whole_b, wb, wb_o, where[1])


def start_kernel(where, dna, cot, keep, send, rows, held, held_cot, sems):
    core = where[1]
    part = dna.shape[1] // 4
    width = cot.shape[2]
    tiles = rows.shape[0]
    order = ((send, 1 - core), (keep, core))
    copies = []
    for at, (_, window) in enumerate(order):
        copies.append(pltpu.make_async_copy(dna.at[window], held.at[at], sems.at[at]))
    copies.append(pltpu.make_async_copy(cot, held_cot, sems.at[2]))
    for copy in (copies[0], copies[2], copies[1]):
        copy.start()
    for at, (out, window) in enumerate(order):
        copies[at].wait()
        v = held[at].astype(F32)
        v = v * lax.rsqrt(jnp.mean(v * v, axis=-1, keepdims=True) + EPS)
        for tile in range(tiles):
            rows[tile] = v[:, 128 * tile : 128 * tile + 128]
        for plane in range(4):
            taken = [rows[tile, pl.ds(plane, part, stride=4), :] for tile in range(tiles)]
            taken = jnp.concatenate(taken, axis=1).astype(BF16)
            out[part * plane : part * plane + part, :] = taken
    copies[2].wait()
    for out, window in order:
        out[4 * part :, 0:width] = held_cot[window]


def split_share(share):
    return share * 4 // 5, share // 5


def pack_kernel(where, keep, other, b0, b1, b2, b3, shares, cots):
    chip, core = where[0], where[1]
    part = keep.shape[0] // 5
    share = keep.shape[1] // 4
    width = cots.shape[1]
    main, tail = split_share(share)
    for source, position in ((keep, core), (other, 1 - core)):
        for plane in range(4):
            at = pl.multiple_of(2 * part * plane + part * position, 16)
            for j in range(4):
                shares[j, pl.ds(at, part), :] = source[
                    part * plane : part * plane + part, share * j : share * j + share
                ]
        cots[pl.ds(pl.multiple_of(part * position, 16), part), :] = source[4 * part :, 0:width]
    block = 2 * part
    rest = width - main
    for step, out in enumerate((b0, b1, b2, b3)):
        rows = shares[chip ^ step]
        out[0 : 4 * block, :] = rows[:, 0:main]
        tails = [rows[block * plane : block * plane + block, main:share] for plane in range(4)]
        out[4 * block : 5 * block, :] = jnp.concatenate(tails, axis=1)
        out[5 * block : 6 * block, :] = cots[:, 0:main]
        out[6 * block :, 0:rest] = cots[0:part, main:width]
        out[6 * block :, rest : 2 * rest] = cots[part:block, main:width]


def open_plane(packed, plane, rows, tail):
    return jnp.concatenate(
        [
            packed[rows * plane : rows * plane + rows, :],
            packed[4 * rows : 5 * rows, tail * plane : tail * plane + tail],
        ],
        axis=1,
    )


def over_tails(column, rows, tail):
    parts = [column[rows * plane : rows * plane + rows] for plane in range(4)]
    parts = [jnp.broadcast_to(v, (rows, tail)) for v in parts]
    return jnp.concatenate(parts, axis=1)


def to_row(column):
    wide = jnp.broadcast_to(column, (column.shape[0], 128))
    if column.shape[0] < 128:
        wide = jnp.concatenate([wide, jnp.zeros((128 - column.shape[0], 128), F32)], axis=0)
    return jnp.transpose(wide)[0:8, :]


def to_column(row, rows):
    wide = jnp.concatenate([row] * 16, axis=0)
    return jnp.transpose(wide)[0:rows, 0:1]


def share_row(vector, index):
    whole = vector[...].reshape(1, vector.shape[0])
    share = vector.shape[0] // 4
    if isinstance(index, int):
        return whole[:, share * index : share * index + share]
    taken = whole[:, 0:share]
    for j in range(1, 4):
        taken = jnp.where(index == j, whole[:, share * j : share * j + share], taken)
    return taken


def slope_kernel(where, b0, b1, b2, b3, gain, slope):
    chip = where[0]
    block = slope.shape[1] // 4
    share = gain.shape[0] // 4
    main, tail = split_share(share)
    g = share_row(gain, chip)
    for step, b in enumerate((b0, b1, b2, b3)):
        at = pl.multiple_of(block * (chip ^ step), 32)
        for plane in range(4):
            n = open_plane(b, plane, block, tail).astype(F32)
            slope[plane, pl.ds(at, block), :] = gelu_slope(n * g) * g * n


def first_kernel(
    where, b0, b1, b2, b3, gain, whole_a, whole_b,
    own, s1, s2, s3, planes, cots, cols, total,
):
    chip = where[0]
    block = planes.shape[1] // 4
    part = block // 2
    share = gain.shape[0] // 4
    main, tail = split_share(share)
    rest = cots.shape[1] - main
    for step, b in enumerate((b0, b1, b2, b3)):
        at = pl.multiple_of(block * (chip ^ step), 32)
        for plane in range(4):
            planes[plane, pl.ds(at, block), :] = open_plane(b, plane, block, tail)
        cots[pl.ds(at, block), 0:main] = b[5 * block : 6 * block, :]
        low = pl.multiple_of(at + part, 16)
        cots[pl.ds(at, part), main:] = b[6 * block :, 0:rest]
        cots[pl.ds(low, part), main:] = b[6 * block :, rest : 2 * rest]
    length = 4 * block
    g = share_row(gain, chip)
    act = [gelu_tanh(planes[plane].astype(F32) * g) for plane in range(4)]
    pa = 0.5 * (act[0] + act[1])
    pb = 0.5 * (act[1] + act[2])
    pc = 0.5 * (act[2] + act[3])
    pd = 0.5 * (act[3] + later(act[0]))
    pd_early = 0.5 * (earlier(act[3]) + act[0])
    even = (earlier(pc), pd_early, pa, pb, pc)
    odd = (pa, pb, pc, pd, later(pa))
    for t in range(5):
        cols[t, 0:length, :] = even[t].astype(BF16)
        cols[t, length : 2 * length, :] = odd[t].astype(BF16)
    acc = dot(cols[0], whole_a[0])
    for t in range(1, 5):
        acc = acc + dot(cols[t], whole_a[t])
    total[0] = acc[0:length]
    total[1] = acc[length : 2 * length]
    c = cots[...]
    p = [dot_t(c, whole_b[t]) for t in range(5)]
    total[2] = 0.5 * (later(p[0]) + p[1] + p[2] + earlier(p[3] + p[4]))
    total[3] = 0.5 * (later(p[0] + p[1]) + p[2] + p[3] + earlier(p[4]))
    for step, out in enumerate((own, s1, s2, s3)):
        at = pl.multiple_of(block * (chip ^ step), 32)
        for kind in range(2):
            for half in range(2):
                out[kind, block * half : block * half + block, :] = total[
                    2 * kind + half, pl.ds(at, block), :
                ].astype(out.dtype)


def second_kernel(where, own, r1, r2, r3, bias, mid, send, kept, back):
    chip, low = where[0], where[2] % 2
    value = own[0] + r1[0].astype(F32) + r2[0].astype(F32) + r3[0].astype(F32) + bias[...].reshape(1, bias.shape[0])
    mid[...] = value.astype(BF16)
    send[0] = value.astype(BF16)
    back[chip] = own[1]
    for step, r in ((1, r1), (2, r2), (3, r3)):
        back[chip ^ step] = r[1].astype(F32)
    for high in range(2):
        send[1 + high] = back[2 * high + 1 - low].astype(BF16)
        kept[high] = back[2 * high + low]


def third_kernel(where, mid, near, kept, send, keep):
    high = where[2] // 2
    send[0] = mid[...]
    send[1] = near[0]
    send[2] = (kept[1 - high] + near[2 - high].astype(F32)).astype(BF16)
    keep[...] = kept[high] + near[1 + high].astype(F32)


def fourth_kernel(
    where, pair, far, keep, gain, a0, a1, a2, a3, grad_n, normed, scale, inner, mids, acts
):
    chip, layer = where[0], where[2]
    mids[layer] = pair[0].astype(F32)
    mids[layer ^ 1] = pair[1].astype(F32)
    mids[layer ^ 2] = far[0].astype(F32)
    mids[layer ^ 3] = far[1].astype(F32)
    squares = sum(mids[j] * mids[j] for j in range(4))
    width = gain.shape[0]
    root = lax.rsqrt(jnp.sum(squares, axis=-1, keepdims=True) / width + EPS)
    for j in range(4):
        acts[j] = gelu_tanh(mids[j] * root * share_row(gain, j)).astype(BF16)
    for step, out in enumerate((a0, a1, a2, a3)):
        out[...] = acts[chip ^ step]
    n = mids[layer] * root
    g = share_row(gain, layer)
    back = keep[...] + far[2].astype(F32)
    grad = back * gelu_slope(n * g) * g
    grad_n[...] = grad
    normed[...] = n
    scale[...] = jnp.broadcast_to(root, scale.shape)
    inner[...] = to_row(jnp.sum(grad * n, axis=-1, keepdims=True))


def fifth_kernel(where, a0, a1, a2, a3, grad_n, normed, scale, i0, i1, t0, t1, t2, t3, *, width):
    inner = to_column(i0[...] + i1[...], grad_n.shape[0]) * (1.0 / width)
    grad = (scale[:, 0:1] * (grad_n[...] - normed[...] * inner)).astype(BF16)
    for a, t in ((a0, t0), (a1, t1), (a2, t2), (a3, t3)):
        t[0] = a[...]
        t[1] = grad


def sixth_kernel(where, t0, t1, t2, t3, whole_a, slope, send, kept, inner, rows, total):
    chip, low = where[0], where[2] % 2
    block = t0.shape[1] // 2
    length = 4 * block
    share = whole_a.shape[1]
    main, tail = split_share(share)
    for step, t in enumerate((t0, t1, t2, t3)):
        at = pl.multiple_of(block * (chip ^ step), 32)
        for half in range(2):
            rows[pl.ds(pl.multiple_of(length * half + at, 32), block), :] = t[
                1, block * half : block * half + block, :
            ]
    u = rows[...]
    p = [dot_t(u, whole_a[t]) for t in range(5)]
    e = [v[0:length] for v in p]
    o = [v[length : 2 * length] for v in p]
    total[0] = 0.5 * (o[0] + e[1] + e[2] + earlier(o[3] + o[4]))
    total[1] = 0.5 * (o[0] + o[1] + e[2] + e[3] + earlier(o[4]))
    total[2] = 0.5 * (later(e[0]) + o[1] + o[2] + e[3] + e[4])
    total[3] = 0.5 * (later(e[0] + e[1]) + o[2] + o[3] + e[4])
    lanes = lax.broadcasted_iota(jnp.int32, (length, 128), 1)
    wide = jnp.zeros((length, 128), F32)
    for plane in range(4):
        column = jnp.sum(total[plane] * slope[plane], axis=-1, keepdims=True)
        wide = jnp.where(lanes == plane, column, wide)
    inner[...] = jnp.transpose(wide)[0:8, :]
    for high in range(2):
        away = pl.multiple_of(block * (2 * high + 1 - low), 32)
        here = pl.multiple_of(block * (2 * high + low), 32)
        for out, start in ((send, away), (kept, here)):
            tails = []
            for plane in range(4):
                taken = total[plane, pl.ds(start, block), :]
                out[high, block * plane : block * plane + block, :] = taken[:, 0:main].astype(out.dtype)
                tails.append(taken[:, main:share])
            out[high, 4 * block : 5 * block, :] = jnp.concatenate(tails, axis=1).astype(out.dtype)


def out_kernel(where, t0, t1, t2, t3, whole_b, own, s1, s2, s3, rows, total):
    chip = where[0]
    block = t0.shape[1] // 2
    for step, t in enumerate((t0, t1, t2, t3)):
        at = pl.multiple_of(block * (chip ^ step), 32)
        for half in range(2):
            rows[half, pl.ds(at, block), :] = t[0, block * half : block * half + block, :].astype(F32)
    even, odd = rows[0], rows[1]
    qe = 0.5 * (even + odd)
    qo = 0.5 * (odd + later(even))
    qo_early = 0.5 * (earlier(odd) + even)
    cols = (earlier(qe), qo_early, qe, qo, later(qe))
    acc = dot(cols[0].astype(BF16), whole_b[0])
    for t in range(1, 5):
        acc = acc + dot(cols[t].astype(BF16), whole_b[t])
    total[...] = acc
    for step, out in enumerate((own, s1, s2, s3)):
        at = pl.multiple_of(block * (chip ^ step), 32)
        out[...] = total[pl.ds(at, block), :].astype(out.dtype)


def add_out_kernel(where, own, r1, r2, r3, bias, mine, send, total):
    core = where[1]
    part = own.shape[0] // 2
    value = own[...] + r1[...].astype(F32) + r2[...].astype(F32) + r3[...].astype(F32)
    total[...] = (value + bias[...].reshape(1, bias.shape[0])).astype(BF16)
    mine[...] = total[pl.ds(pl.multiple_of(part * core, 16), part), :]
    send[...] = total[pl.ds(pl.multiple_of(part * (1 - core), 16), part), :]


def put_out_kernel(where, mine, other, out):
    core = where[1]
    out[core] = mine[...]
    out[1 - core] = other[...]


def seventh_kernel(where, kept, near, send, keep):
    high = where[2] // 2
    send[...] = (kept[1 - high] + near[1 - high].astype(F32)).astype(BF16)
    keep[...] = kept[high] + near[high].astype(F32)


def eighth_kernel(
    where, keep, far, b0, b1, b2, b3, gain, i0, i1, same, cross, total, column, *, width
):
    chip, core, layer = where[0], where[1], where[2]
    rows, main = keep.shape
    block = rows // 5
    part = block // 2
    tail = main // 4
    wide = jnp.concatenate([i0[...] + i1[...]] * 16, axis=0)
    column[...] = jnp.transpose(wide) * (1.0 / width)
    taken = column[pl.ds(pl.multiple_of(block * layer, 32), block), :]
    inner = jnp.concatenate([taken[:, plane : plane + 1] for plane in range(4)], axis=0)
    step = chip ^ layer
    low = jnp.where(step == 0, b0[0:rows], b1[0:rows])
    high = jnp.where(step == 2, b2[0:rows], b3[0:rows])
    n = jnp.where(step < 2, low, high).astype(F32)
    g = share_row(gain, chip)
    back = keep[...] + far[...].astype(F32)
    sides = (
        (0, 4 * block, g[:, 0:main], inner),
        (4 * block, rows, jnp.concatenate([g[:, main:]] * 4, axis=1), over_tails(inner, block, tail)),
    )
    for start, stop, weight, mean in sides:
        v = n[start:stop]
        total[start:stop, :] = back[start:stop] * gelu_slope(v * weight) * weight - v * mean
    for plane in range(5):
        at = slice(part * plane, part * plane + part)
        lower = total[block * plane : block * plane + part, :].astype(BF16)
        upper = total[block * plane + part : block * plane + block, :].astype(BF16)
        same[at, :] = jnp.where(core == 0, lower, upper)
        cross[at, :] = jnp.where(core == 0, upper, lower)


def last_kernel(where, same, cross, dna, out, rows):
    core = where[1]
    part = dna.shape[1] // 4
    share = out.shape[2]
    main, tail = split_share(share)
    for x, window in ((same, core), (cross, 1 - core)):
        v = dna[window].astype(F32)
        root = lax.rsqrt(jnp.mean(v * v, axis=-1, keepdims=True) + EPS)
        for plane in range(4):
            taken = open_plane(x, plane, part, tail).astype(F32)
            for tile in range(rows.shape[0]):
                lanes = min(128, share - 128 * tile)
                rows[tile, pl.ds(plane, part, stride=4), 0:lanes] = taken[
                    :, 128 * tile : 128 * tile + lanes
                ]
        whole = jnp.concatenate([rows[tile] for tile in range(rows.shape[0])], axis=1)
        out[window] = (whole[:, 0:share] * root).astype(BF16)


def stationary(dna_features, gain_a, conv_a, bias_a, gain_b, conv_b, bias_b, grad_out):
    chips = lax.axis_size("ch")
    place = lax.axis_index("seq")
    layer = lax.axis_index("ch")
    chip, core = place // 2, place % 2
    where = jnp.stack([chip, core, layer]).astype(jnp.int32)
    windows, rows_in, width_in = dna_features.shape
    width_mid = gain_b.shape[0]
    share_in, share_mid, share_out = width_in // chips, bias_a.shape[0], bias_b.shape[0]
    part = rows_in // 4
    block = 2 * part
    length = chips * block
    taps = conv_a.shape[0]
    steps = range(1, chips)

    other_a = swap(conv_a, "seq", 1)
    other_b = swap(conv_b, "seq", 1)
    half = ((5 * part, width_in), BF16)
    keep, send = call(
        start_kernel,
        [half] * 2,
        where,
        (dna_features, grad_out),
        [
            ((width_in // 128, rows_in, 128), F32),
            (dna_features.shape, BF16),
            (grad_out.shape, BF16),
            pltpu.SemaphoreType.DMA((3,)),
        ],
        place=pl.ANY,
    )
    other = swap(send, "seq", 1)
    main, tail = split_share(share_in)
    packed = ((13 * part, main), BF16)
    blocks = call(
        pack_kernel,
        [packed] * 4,
        where,
        (keep, other),
        [((chips, 4 * block, share_in), BF16), ((block, share_out), BF16)],
    )
    whole_a, whole_b = call(
        join_kernel,
        [((taps, share_in, share_mid), BF16), ((taps, share_mid, share_out), BF16)],
        where,
        (conv_a, other_a, conv_b, other_b),
        after=blocks[:1],
    )
    blocks = [blocks[0]] + [swap(blocks[d], "seq", 2 * d) for d in steps]

    pair = (2, 2 * block, share_mid)
    sums = call(
        first_kernel,
        [(pair, F32)] + [(pair, BF16)] * 3,
        where,
        (*blocks, gain_a, whole_a, whole_b),
        [
            ((4, length, share_in), BF16),
            ((length, share_out), BF16),
            ((taps, 2 * length, share_in), BF16),
            ((4, length, share_mid), F32),
        ],
    )
    sums = [sums[0]] + [swap(sums[d], "seq", 2 * d) for d in steps]
    (slope,) = call(
        slope_kernel,
        [((4, length, share_in), F32)],
        where,
        (*blocks, gain_a),
        after=sums[:1],
    )
    one = (2 * block, share_mid)
    mid, send, kept = call(
        second_kernel,
        [(one, BF16), ((3,) + one, BF16), ((2,) + one, F32)],
        where,
        (*sums, bias_a),
        [((chips,) + one, F32)],
        after=[slope],
    )
    near = swap(send, "ch", 1)
    pair_mid, keep = call(
        third_kernel, [((3,) + one, BF16), (one, F32)], where, (mid, near, kept)
    )
    far = swap(pair_mid, "ch", 2)
    lane = (2 * block, 128)
    row = (8, 128)
    *acts, grad_n, normed, scale, inner = call(
        fourth_kernel,
        [(one, BF16)] * 4 + [(one, F32), (one, F32), (lane, F32), (row, F32)],
        where,
        (pair_mid, far, keep, gain_b),
        [((chips,) + one, F32), ((chips,) + one, BF16)],
    )
    inner = inner + swap(inner, "ch", 1)
    inner_far = swap(inner, "ch", 2)
    rest = call(
        functools.partial(fifth_kernel, width=width_mid),
        [(pair, BF16)] * 4,
        where,
        (*acts, grad_n, normed, scale, inner, inner_far),
    )
    rest = [rest[0]] + [swap(rest[d], "seq", 2 * d) for d in steps]

    quarter = (5 * block, main)
    send, kept, inner = call(
        sixth_kernel,
        [((2,) + quarter, BF16), ((2,) + quarter, F32), (row, F32)],
        where,
        (*rest, whole_a, slope),
        [
            ((2 * length, share_mid), BF16),
            ((4, length, share_in), F32),
        ],
    )
    near = swap(send, "ch", 1)
    inners = [swap(inner, "seq", 2 * d) for d in steps]
    outs = call(
        out_kernel,
        [((block, share_out), F32)] + [((block, share_out), BF16)] * 3,
        where,
        (*rest, whole_b),
        [
            ((2, length, share_mid), F32),
            ((length, share_out), F32),
        ],
    )
    send, keep = call(
        seventh_kernel,
        [(quarter, BF16), (quarter, F32)],
        where,
        (kept, near),
        after=[outs[0], *inners],
    )
    far = swap(send, "ch", 2)
    inner = (inner + inners[0]) + (inners[1] + inners[2])
    inner = inner + swap(inner, "ch", 1)
    inner_far = swap(inner, "ch", 2)
    outs = [outs[0]] + [swap(outs[d], "seq", 2 * d) for d in steps]
    same, cross = call(
        functools.partial(eighth_kernel, width=width_in),
        [((5 * part, main), BF16)] * 2,
        where,
        (keep, far, *blocks, gain_a, inner, inner_far),
        [(quarter, F32), ((128, 128), F32)],
        after=outs[1:],
    )
    last = same
    same, cross = transpose_chips(same, 0), transpose_chips(cross, 1)
    mine, send = call(
        add_out_kernel,
        [((part, share_out), BF16)] * 2,
        where,
        (*outs, bias_b),
        [((block, share_out), BF16)],
        after=[last],
    )
    other = swap(send, "seq", 1)
    (pooled_out,) = call(
        put_out_kernel, [(grad_out.shape, BF16)], where, (mine, other)
    )
    (input_grad,) = call(
        last_kernel,
        [((windows, rows_in, share_in), BF16)],
        where,
        (same, cross, dna_features),
        [((-(-share_in // 128), rows_in, 128), F32)],
    )
    return (pooled_out, input_grad)


def fits(mesh_shape, args):
    places, layers = mesh_shape["seq"], mesh_shape["ch"]
    windows, rows = args[0].shape[0], args[0].shape[1]
    share_in, share_out = args[0].shape[2] // layers, args[7].shape[2] // layers
    main, tail = split_share(share_in)
    even = main + tail == share_in and main % 256 == 0 and 2 * (share_out - main) == main
    return even and places == 2 * layers and layers == 4 and windows == 2 and rows == 64 * places


def solution(mesh):
    in_specs = (
        P(None, "seq", None),
        P(),
        P(None, "seq", "ch"),
        P("ch"),
        P(),
        P(None, "seq", "ch"),
        P("ch"),
        P(None, "seq", "ch"),
    )
    out_specs = (P(None, "seq", "ch"), P(None, "seq", "ch"))
    def run(*args):
        plan = stationary if fits(mesh.shape, args) else per_device
        return jax.shard_map(
            plan, mesh=mesh, in_specs=in_specs, out_specs=out_specs, check_vma=False
        )(*args)

    return run
```
